32 devices in a mesh: dp: 8 (over z, y), seq: 4 (over x, core).
Axes of the slice: x: 2, y: 2, z: 4, core: 2. Of those that a mesh axis runs over, the one named last changes fastest.
Arguments:
- tokens: bfloat16 [8, 1152, 1024], P('dp', 'seq'), may hold values from -6 to 6
- segment_ids: int32 [8, 1152], P('dp'), may hold values from 0 to 3, never falling along the last dimension, each value on 1 to 640 neighbouring positions
- qkv_weight: bfloat16 [1024, 3072], P(('dp', 'seq')), may hold values from -0.1875 to 0.1875
- query_bias: bfloat16 [1024], P(('dp', 'seq')), may hold values from -1.75 to 1.75
- value_bias: bfloat16 [1024], P(('dp', 'seq')), may hold values from -0.625 to 0.625
- out_weight: bfloat16 [1024, 1024], P(('dp', 'seq')), may hold values from -1 to 1
- out_bias: bfloat16 [1024], P(('dp', 'seq')), may hold values from -3 to 3
- first_gain: bfloat16 [1024], P(('dp', 'seq')), may hold values from 0.25 to 1.75
- first_shift: bfloat16 [1024], P(('dp', 'seq')), may hold values from -3 to 3
- up_weight: bfloat16 [1024, 4096], P(('dp', 'seq')), may hold values from -0.1875 to 0.1875
- up_bias: bfloat16 [4096], P(('dp', 'seq')), may hold values from -3 to 3
- down_weight: bfloat16 [4096, 1024], P(('dp', 'seq')), may hold values from -0.09375 to 0.09375
- down_bias: bfloat16 [1024], P(('dp', 'seq')), may hold values from -3 to 3
- second_gain: bfloat16 [1024], P(('dp', 'seq')), may hold values from 0.25 to 1.75
- second_shift: bfloat16 [1024], P(('dp', 'seq')), may hold values from -3 to 3
- cotangent: bfloat16 [8, 1152, 1024], P('dp', 'seq'), may hold values from -6 to 6
Outputs:
- output: bfloat16 [8, 1152, 1024], P('dp', 'seq')
- tokens_grad: bfloat16 [8, 1152, 1024], P('dp', 'seq')
- qkv_weight_grad: float32 [1024, 3072], P(('dp', 'seq'))
- query_bias_grad: float32 [1024], P(('dp', 'seq'))
- value_bias_grad: float32 [1024], P(('dp', 'seq'))
- out_weight_grad: float32 [1024, 1024], P(('dp', 'seq'))
- out_bias_grad: float32 [1024], P(('dp', 'seq'))
- first_gain_grad: float32 [1024], P(('dp', 'seq'))
- first_shift_grad: float32 [1024], P(('dp', 'seq'))
- up_weight_grad: float32 [1024, 4096], P(('dp', 'seq'))
- up_bias_grad: float32 [4096], P(('dp', 'seq'))
- down_weight_grad: float32 [4096, 1024], P(('dp', 'seq'))
- down_bias_grad: float32 [1024], P(('dp', 'seq'))
- second_gain_grad: float32 [1024], P(('dp', 'seq'))
- second_shift_grad: float32 [1024], P(('dp', 'seq'))
The draws below stay inside these ranges and needn't reach their ends.
Inputs may be any that keep to these rules, and one draw needn't show every extreme that they name: `segment_ids`: in each sequence the document numbers never fall along the tokens; a document spans 1 to 640 tokens, and some document spans exactly 640.
All inputs are finite; a program needn't handle non-finite values.
Results may differ from the reference program's by a relative error of at most 0.014.
Values may be sent and summed in bfloat16 or wider, within the bound.
No kernel may reach another device: no remote copies, remote signals or barrier semaphores. Data moves between devices by JAX's collectives and lax.ppermute only.
A program may use at most 192 MiB of HBM per device.

```python
import math
import jax
import jax.numpy as jnp
import numpy as np
from jax import lax

D = 1024
HEADS = 16
HEAD_DIM = 64
FF = 4096
LEN = 1152
SEG_MOST = 640
SEG_COUNT = 4
SEQS = 8


def level_of(key, shape, cuts, smallest, largest):
    loudness, own = 1.0, jax.random.fold_in(key, 6)
    for dim, parts in cuts:
        draws = jnp.exp(jax.random.uniform(jax.random.fold_in(own, dim), (parts,), jnp.float32, smallest / len(cuts), largest / len(cuts)))
        loudness = loudness * jnp.repeat(draws, shape[dim] // parts).reshape([-1 if axis == dim else 1 for axis in range(len(shape))])
    return loudness


def profile(count, total, bound, lean):
    loads = [(1 << 20) // math.isqrt(standing ** lean) + 1 for standing in range(2, count + 1)]
    rest, given = total - bound - (count - 1), [1] * (count - 1)
    while rest > 0:
        movable = [i for i in range(count - 1) if given[i] < bound]
        whole, budget = sum([loads[i] for i in movable]), rest
        for i in movable:
            extra = min(bound - given[i], max(1, budget * loads[i] // whole), rest)
            given[i] = given[i] + extra
            rest = rest - extra
    return np.array([bound] + given)


def ragged(rng, count, total, bound, lean):
    if count == 2:
        one = jax.random.randint(rng, (), max(1, total - bound), min(bound, total - 1) + 1)
        return jnp.stack([one, total - one])
    lengths = jnp.asarray(profile(count, total, bound, lean), jnp.int32)
    pairs = (count - 1) // 2
    giver, taker = lengths[1:1 + 2 * pairs:2], lengths[2:2 + 2 * pairs:2]
    room = jnp.minimum(giver - 1, bound - taker)
    moved = jax.random.randint(jax.random.fold_in(rng, 1), (pairs,), 0, 1 << 20) % (room + 1)
    lengths = lengths.at[1:1 + 2 * pairs:2].set(giver - moved).at[2:2 + 2 * pairs:2].set(taker + moved)
    return lengths[jax.random.permutation(jax.random.fold_in(rng, 2), count)]


def gaussian(rng, shape, deviation, limit, shards=(), kind=jnp.bfloat16):
    level = level_of(rng, shape, shards, -0.22, 0.18) if shards else 1.0
    array = jax.random.normal(rng, shape, jnp.float32) * deviation * level
    return jnp.minimum(jnp.maximum(array, -limit), limit).astype(kind)


def setup_inputs(seed: int = 0) -> dict:
    streams_of = jax.random.split(jax.random.key(seed), 17)
    return {
        "tokens": gaussian(streams_of[0], (SEQS, LEN, D), 1.0, 6.0, ((0, 8), (1, 4))),
        "segment_ids": jax.vmap(lambda own: jnp.searchsorted(jnp.cumsum(ragged(own, SEG_COUNT, LEN, SEG_MOST, 2)), jnp.arange(LEN), side="right"))(jax.random.split(streams_of[1], SEQS)).reshape((SEQS, LEN)).astype(jnp.int32),
        "qkv_weight": gaussian(streams_of[2], (D, 3 * D), D ** -0.5, 0.1875, ((0, 32),)),
        "query_bias": gaussian(streams_of[3], (D,), 0.3, 1.75, ((0, 32),)),
        "value_bias": gaussian(streams_of[4], (D,), 0.1, 0.625, ((0, 32),)),
        "out_weight": gaussian(streams_of[5], (D, D), (D // 32) ** -0.5, 1.0, ((0, 32),)),
        "out_bias": gaussian(streams_of[6], (D,), 0.5, 3.0, ((0, 32),)),
        "first_gain": jnp.clip(1.0 + 0.15 * jax.random.normal(streams_of[7], (D,), jnp.float32), 0.25, 1.75).astype(jnp.bfloat16),
        "first_shift": gaussian(streams_of[8], (D,), 0.5, 3.0, ((0, 32),)),
        "up_weight": gaussian(streams_of[9], (D, FF), D ** -0.5, 0.1875, ((0, 32),)),
        "up_bias": gaussian(streams_of[10], (FF,), 0.5, 3.0, ((0, 32),)),
        "down_weight": gaussian(streams_of[11], (FF, D), FF ** -0.5, 0.09375, ((0, 32),)),
        "down_bias": gaussian(streams_of[12], (D,), 0.5, 3.0, ((0, 32),)),
        "second_gain": jnp.clip(1.0 + 0.15 * jax.random.normal(streams_of[13], (D,), jnp.float32), 0.25, 1.75).astype(jnp.bfloat16),
        "second_shift": gaussian(streams_of[14], (D,), 0.5, 3.0, ((0, 32),)),
        "cotangent": gaussian(streams_of[15], (SEQS, LEN, D), 1.0, 6.0, ((0, 8), (1, 4))),
    }


@jax.custom_vjp
def low(v):
    return lax.optimization_barrier(v.astype(jnp.bfloat16)).astype(jnp.float32)

@jax.custom_vjp
def low_back(v):
    return v

def low_keep(v):
    return (low(v), None)

def low_pass(kept, grad):
    return (grad,)

def back_keep(v):
    return (v, None)

def back_low(kept, grad):
    return (low(grad),)
low.defvjp(low_keep, low_pass)
low_back.defvjp(back_keep, back_low)
EPSILON = 1e-06
MASKED = -1e+30

def product(left, right):
    return jnp.dot(left, right, precision=lax.Precision.HIGHEST, preferred_element_type=jnp.float32)

def layer_norm(value, gain, shift):
    mean = lax.optimization_barrier(jnp.mean(value, axis=-1, keepdims=True))
    centered = value - mean
    variance = lax.optimization_barrier(jnp.mean(centered * centered, axis=-1, keepdims=True))
    return centered * lax.rsqrt(variance + EPSILON) * gain + shift

def attention(projected, segments):
    length = projected.shape[0]
    queries = projected[:, :D].reshape(length, HEADS, HEAD_DIM)
    keys = projected[:, D:2 * D].reshape(length, HEADS, HEAD_DIM)
    values = projected[:, 2 * D:].reshape(length, HEADS, HEAD_DIM)
    scores = jnp.einsum('qhd,khd->hqk', queries, keys, precision=lax.Precision.HIGHEST) * HEAD_DIM ** (-0.5)
    scores = low_back(scores)
    same = segments[:, None] == segments[None, :]
    scores = jnp.where(same[None], scores, MASKED)
    shares = low(jax.nn.softmax(scores, axis=-1))
    mixed = jnp.einsum('hqk,khd->qhd', shares, values, precision=lax.Precision.HIGHEST)
    return mixed.reshape(length, D)

def forward(rows, segments, qkv_weight, query_bias, value_bias, out_weight, out_bias, first_gain, first_shift, up_weight, up_bias, down_weight, down_bias, second_gain, second_shift):
    bias = jnp.concatenate([query_bias, jnp.zeros_like(query_bias), value_bias])
    projected = low(low_back(product(rows, qkv_weight) + bias))
    mixed = low(low_back(attention(projected, segments)))
    branch = low_back(product(mixed, out_weight) + out_bias)
    first = layer_norm(rows + branch, first_gain, first_shift)
    preact = low_back(product(low(first), up_weight) + up_bias)
    hidden = low(jax.nn.gelu(preact, approximate=False))
    second = low_back(product(hidden, down_weight) + down_bias)
    return layer_norm(first + second, second_gain, second_shift)

def reference(tokens, segment_ids, qkv_weight, query_bias, value_bias, out_weight, out_bias, first_gain, first_shift, up_weight, up_bias, down_weight, down_bias, second_gain, second_shift, cotangent):
    params = tuple((value.astype(jnp.float32) for value in (qkv_weight, query_bias, value_bias, out_weight, out_bias, first_gain, first_shift, up_weight, up_bias, down_weight, down_bias, second_gain, second_shift)))

    def one_sequence(totals, block):
        rows, segments, grad_out = block

        def forward_rows(rows_in, *weights):
            return forward(rows_in, segments, *weights)
        result, pullback = jax.vjp(forward_rows, rows.astype(jnp.float32), *params)
        grads = pullback(grad_out.astype(jnp.float32))
        summed = tuple((total + grad for total, grad in zip(totals, grads[1:])))
        return (summed, (result.astype(jnp.bfloat16), grads[0].astype(jnp.bfloat16)))
    initial = tuple((jnp.zeros(value.shape, jnp.float32) for value in params))
    totals, (output, tokens_grad) = lax.scan(one_sequence, initial, (tokens, segment_ids, cotangent))
    qkv_weight_grad, query_bias_grad, value_bias_grad, out_weight_grad, out_bias_grad, first_gain_grad, first_shift_grad, up_weight_grad, up_bias_grad, down_weight_grad, down_bias_grad, second_gain_grad, second_shift_grad = totals
    return (output, tokens_grad, qkv_weight_grad, query_bias_grad, value_bias_grad, out_weight_grad, out_bias_grad, first_gain_grad, first_shift_grad, up_weight_grad, up_bias_grad, down_weight_grad, down_bias_grad, second_gain_grad, second_shift_grad)
```

```python
from functools import partial

import jax
import jax.numpy as jnp
from jax import lax
from jax.experimental import pallas as pl
from jax.experimental.pallas import tpu as pltpu
from jax.sharding import PartitionSpec as P

HEADS = 16
HEAD_DIM = 64
EPSILON = 1e-06
MASKED = -1e30
CORES = 2
F32 = jnp.float32
BF16 = jnp.bfloat16
DN_T = (((1,), (1,)), ((), ()))
DN_L = (((0,), (0,)), ((), ()))


def matmul(left, right):
    return jnp.dot(left, right, preferred_element_type=F32)


def left_product(left, right):
    return lax.dot_general(left, right, DN_L, preferred_element_type=F32)


def right_product(left, right):
    return lax.dot_general(left, right, DN_T, preferred_element_type=F32)


def norm_forward(value, gain, shift):
    mean = jnp.mean(value, axis=-1, keepdims=True)
    centered = value - mean
    variance = jnp.mean(centered * centered, axis=-1, keepdims=True)
    factor = lax.rsqrt(variance + EPSILON)
    normed = centered * factor
    return (normed * gain + shift, normed, factor)


def norm_backward(grad, normed, factor, gain):
    scaled = grad * gain
    inner = jnp.mean(scaled, axis=-1, keepdims=True)
    along = jnp.mean(scaled * normed, axis=-1, keepdims=True)
    return (
        factor * (scaled - inner - normed * along),
        jnp.sum(grad * normed, axis=0),
        jnp.sum(grad, axis=0),
    )


class Place:
    def __init__(self, dp, seq):
        self.dp, self.seq = dp, seq
        self.nx = seq // CORES
        self.ny = min(self.nx, dp)
        self.nz = dp // self.ny
        d = lax.axis_index("dp")
        s = lax.axis_index("seq")
        self.d, self.s = d, s
        self.z, self.y = d // self.ny, d % self.ny
        self.x, self.c = s // CORES, s % CORES

    def core(self, a):
        return lax.ppermute(a, "seq", [(i, i ^ 1) for i in range(self.seq)])

    def to_x(self, a, k):
        n = self.nx
        return lax.ppermute(
            a,
            "seq",
            [(i, ((i // CORES + k) % n) * CORES + i % CORES) for i in range(self.seq)],
        )

    def to_y(self, a, k):
        n = self.ny
        return lax.ppermute(
            a, "dp", [(i, i // n * n + (i % n + k) % n) for i in range(self.dp)]
        )

    def to_z(self, a, k):
        n, m = self.nz, self.ny
        return lax.ppermute(
            a, "dp", [(i, (i // m + k) % n * m + i % m) for i in range(self.dp)]
        )

    def pair(self, own, other, axis):
        first = jnp.where(self.c == 0, own, other)
        second = jnp.where(self.c == 0, other, own)
        return jnp.concatenate([first, second], axis=axis)


def put(buffer, block, index):
    return lax.dynamic_update_slice_in_dim(buffer, block[None], index, 0)


def take(buffer, index):
    return lax.dynamic_index_in_dim(buffer, index, 0, keepdims=False)


def exchange_seq(place, blocks):
    n = place.nx
    view = blocks.reshape(n, CORES, *blocks.shape[1:])
    out = jnp.zeros((n, CORES, *blocks.shape[1:]), blocks.dtype)
    for k in range(n):
        peer = (place.x + k) % n
        send = take(view, peer)
        if k:
            send = place.to_x(send, k)
        source = (place.x - k) % n
        mine = take(send, place.c)
        other = place.core(take(send, 1 - place.c))
        out = put(out, place.pair(mine[None], other[None], 0), source)
    return out.reshape(blocks.shape)


def gather_dp(place, block):
    ny, nz = place.ny, place.nz
    out = jnp.zeros((nz * ny, *block.shape), block.dtype)
    here = block
    for k in range(nz):
        z = (place.z - k) % nz
        out = put(out, here, z * ny + place.y)
        for j in range(1, ny):
            out = put(out, place.to_y(here, j), z * ny + (place.y - j) % ny)
        if k < nz - 1:
            here = place.to_z(here, 1)
    return out.reshape(nz * ny * block.shape[0], *block.shape[1:])


def scatter_dp(place, grads):
    ny, nz = place.ny, place.nz
    view = grads.astype(BF16).reshape(nz * ny, grads.shape[0] // (nz * ny), *grads.shape[1:])
    total = None
    for k in range(1, nz + 1):
        z = (place.z - k) % nz
        part = take(view, z * ny + place.y).astype(F32)
        for j in range(1, ny):
            sent = place.to_y(take(view, z * ny + (place.y + j) % ny), j)
            part = part + sent.astype(F32)
        if total is not None:
            part = part + place.to_z(total.astype(BF16), 1).astype(F32)
        total = part
    return total


def all_sum(place, value):
    for axis, size in (("seq", place.seq), ("dp", place.dp)):
        bit = 1
        while bit < size:
            value = value + lax.ppermute(value, axis, [(i, i ^ bit) for i in range(size)])
            bit *= 2
    return value


def rows_all(place, rows):
    out = []
    for k in range(place.nx):
        here = rows if k == 0 else place.to_x(rows, (place.nx - k) % place.nx)
        out.append(jnp.concatenate([here, place.core(here)], axis=0))
    return out


def rows_sum(place, parts):
    total = None
    for k in reversed(range(place.nx)):
        low = parts[k].astype(BF16)
        half = low.shape[0] // 2
        both = low[:half].astype(F32) + place.core(low[half:]).astype(F32)
        if k:
            both = place.to_x(both.astype(BF16), k).astype(F32)
        total = both if total is None else total + both
    return total


BLOCK = 384


def attend_kernel(heads, bounds, qkv_ref, seg_row, seg_col, mixed_ref, log_ref):
    length = qkv_ref.shape[0]
    width = heads * HEAD_DIM
    i = pl.program_id(0)
    start = pl.multiple_of(i * BLOCK, BLOCK)
    cols = pl.ds(start, BLOCK)
    seg_q = seg_row[:, cols]
    queries = [
        qkv_ref[cols, h * HEAD_DIM : (h + 1) * HEAD_DIM] * BF16(HEAD_DIM**-0.5)
        for h in range(heads)
    ]

    def step(j, carry):
        rows = pl.ds(pl.multiple_of(j * BLOCK, BLOCK), BLOCK)
        same = seg_col[rows, :] == seg_q
        out = []
        for h in range(heads):
            high, total, acc = carry[h]
            keys = qkv_ref[rows, width + h * HEAD_DIM : width + (h + 1) * HEAD_DIM]
            values = qkv_ref[rows, 2 * width + h * HEAD_DIM : 2 * width + (h + 1) * HEAD_DIM]
            scores = lax.dot_general(keys, queries[h], DN_T, preferred_element_type=F32)
            scores = jnp.where(same, scores, MASKED)
            new = jnp.maximum(high, jnp.max(scores, axis=0, keepdims=True))
            weights = jnp.exp(scores - new)
            fade = jnp.exp(high - new)
            total = total * fade + jnp.sum(weights, axis=0, keepdims=True)
            acc = acc * fade + lax.dot_general(
                values, weights.astype(BF16), DN_L, preferred_element_type=F32
            )
            out.append((new, total, acc))
        return tuple(out)

    first = tuple(
        (
            jnp.full((1, BLOCK), MASKED, F32),
            jnp.zeros((1, BLOCK), F32),
            jnp.zeros((HEAD_DIM, BLOCK), F32),
        )
        for _ in range(heads)
    )
    done = lax.fori_loop(bounds[i], bounds[i + length // BLOCK], step, first)
    mixed = jnp.concatenate([acc / total for _, total, acc in done], axis=0)
    mixed_ref[...] = mixed.T.astype(BF16)
    log_ref[...] = jnp.concatenate([high + jnp.log(total) for high, total, _ in done], axis=0)


def attend_back_kernel(
    heads, bounds, qkv_ref, mixed_ref, grad_ref, log_ref, seg_row, seg_col, out_ref, acc_ref
):
    length = qkv_ref.shape[0]
    width = heads * HEAD_DIM
    scale = HEAD_DIM**-0.5
    i = pl.program_id(0)

    @pl.when(i == 0)
    def _():
        acc_ref[...] = jnp.zeros_like(acc_ref)

    start = pl.multiple_of(i * BLOCK, BLOCK)
    cols = pl.ds(start, BLOCK)
    seg_q = seg_row[:, cols]
    grads_all = grad_ref[cols, :]
    along = (grads_all.astype(F32) * mixed_ref[cols, :].astype(F32)).T
    along = [
        jnp.sum(along[h * HEAD_DIM : (h + 1) * HEAD_DIM], axis=0, keepdims=True)
        for h in range(heads)
    ]
    logs = [log_ref[h : h + 1, cols] for h in range(heads)]
    queries = [
        qkv_ref[cols, h * HEAD_DIM : (h + 1) * HEAD_DIM] * BF16(scale) for h in range(heads)
    ]
    grads = [grads_all[:, h * HEAD_DIM : (h + 1) * HEAD_DIM] for h in range(heads)]

    def step(j, carry):
        rows = pl.ds(pl.multiple_of(j * BLOCK, BLOCK), BLOCK)
        same = seg_col[rows, :] == seg_q
        out, key_parts, value_parts = [], [], []
        for h in range(heads):
            keys = qkv_ref[rows, width + h * HEAD_DIM : width + (h + 1) * HEAD_DIM]
            values = qkv_ref[rows, 2 * width + h * HEAD_DIM : 2 * width + (h + 1) * HEAD_DIM]
            scores = lax.dot_general(keys, queries[h], DN_T, preferred_element_type=F32)
            shares = jnp.exp(jnp.where(same, scores, MASKED) - logs[h])
            shares_grad = lax.dot_general(values, grads[h], DN_T, preferred_element_type=F32)
            score_low = (shares * (shares_grad - along[h])).astype(BF16)
            value_parts.append(matmul(shares.astype(BF16), grads[h]))
            key_parts.append(matmul(score_low, queries[h]))
            out.append(
                carry[h] + lax.dot_general(keys, score_low, DN_L, preferred_element_type=F32)
            )
        acc_ref[rows, :width] += jnp.concatenate(key_parts, axis=1)
        acc_ref[rows, width:] += jnp.concatenate(value_parts, axis=1)
        return tuple(out)

    first = tuple(jnp.zeros((HEAD_DIM, BLOCK), F32) for _ in range(heads))
    done = lax.fori_loop(bounds[i], bounds[i + length // BLOCK], step, first)
    out_ref[cols, :width] = (jnp.concatenate(done, axis=0) * scale).T.astype(BF16)

    @pl.when(i == length // BLOCK - 1)
    def _():
        out_ref[:, width:] = acc_ref[...].astype(BF16)


VMEM = pl.BlockSpec(memory_space=pltpu.VMEM)


def attend(qkv, seg_row, seg_col, bounds, heads):
    length = qkv.shape[0]
    width = heads * HEAD_DIM
    return pl.pallas_call(
        partial(attend_kernel, heads),
        grid_spec=pltpu.PrefetchScalarGridSpec(
            num_scalar_prefetch=1,
            grid=(length // BLOCK,),
            in_specs=[VMEM, VMEM, VMEM],
            out_specs=[
                pl.BlockSpec((BLOCK, width), lambda i, b: (i, 0)),
                pl.BlockSpec((heads, BLOCK), lambda i, b: (0, i)),
            ],
        ),
        out_shape=[
            jax.ShapeDtypeStruct((length, width), BF16),
            jax.ShapeDtypeStruct((heads, length), F32),
        ],
        compiler_params=pltpu.CompilerParams(vmem_limit_bytes=40 << 20),
        cost_estimate=pl.CostEstimate(
            flops=4 * length * length * width,
            bytes_accessed=8 * length * width,
            transcendentals=length * length * heads,
        ),
    )(bounds, qkv, seg_row, seg_col)


def attend_back(qkv, mixed, grad, logs, seg_row, seg_col, bounds, heads):
    length = qkv.shape[0]
    width = heads * HEAD_DIM
    return pl.pallas_call(
        partial(attend_back_kernel, heads),
        grid_spec=pltpu.PrefetchScalarGridSpec(
            num_scalar_prefetch=1,
            grid=(length // BLOCK,),
            in_specs=[VMEM] * 6,
            out_specs=VMEM,
            scratch_shapes=[pltpu.VMEM((length, 2 * width), F32)],
        ),
        out_shape=jax.ShapeDtypeStruct((length, 3 * width), BF16),
        compiler_params=pltpu.CompilerParams(vmem_limit_bytes=40 << 20),
        cost_estimate=pl.CostEstimate(
            flops=10 * length * length * width,
            bytes_accessed=16 * length * width,
            transcendentals=length * length * heads,
        ),
    )(bounds, qkv, mixed, grad, logs, seg_row, seg_col)


def gelu_pair(preact):
    half = 0.5 + 0.5 * lax.erf(preact * (2.0**-0.5))
    slope = half + preact * jnp.exp(-0.5 * preact * preact) * 0.3989422804014327
    return (preact * half).astype(BF16), slope.astype(BF16)


def body(
    dp,
    seq,
    tokens,
    segment_ids,
    qkv_weight,
    query_bias,
    value_bias,
    out_weight,
    out_bias,
    first_gain,
    first_shift,
    up_weight,
    up_bias,
    down_weight,
    down_bias,
    second_gain,
    second_shift,
    cotangent,
):
    place = Place(dp, seq)
    everyone = dp * seq
    me = place.d * seq + place.s
    _, count, width = tokens.shape
    hidden_own = up_weight.shape[1] // seq
    heads = HEADS // seq
    head_cols = heads * HEAD_DIM
    shard = qkv_weight.shape[0]
    ff_shard = down_weight.shape[0]
    length = segment_ids.shape[1]
    rows = tokens.reshape(count, width)

    qkv_blocks = qkv_weight.reshape(shard, 3, seq, head_cols).transpose(2, 0, 1, 3)
    qkv_block = exchange_seq(place, qkv_blocks.reshape(seq, shard, 3 * head_cols))
    full_qkv = gather_dp(place, qkv_block.reshape(seq * shard, 3 * head_cols))

    smalls = (query_bias, value_bias, out_bias, first_gain, first_shift, down_bias, second_gain, second_shift)
    packed = jnp.concatenate([v.reshape(1, shard) for v in smalls] + [up_bias.reshape(-1, shard)], axis=0)
    packed = all_sum(
        place, put(jnp.zeros((everyone, *packed.shape), F32), packed.astype(F32), me)
    )
    vectors = packed[:, : len(smalls)].transpose(1, 0, 2).reshape(len(smalls), 1, width)
    full_query, full_value, bias_out, gain_one, shift_one, bias_down, gain_two, shift_two = vectors
    up_bias_all = packed[:, len(smalls) :].reshape(dp, seq, ff_shard)
    bias_up = lax.dynamic_index_in_dim(up_bias_all, place.s, 1, keepdims=False).reshape(1, hidden_own)

    row_blocks = rows_all(place, rows)
    all_rows = jnp.zeros((place.nx, CORES * count, width), BF16)
    for k, both in enumerate(row_blocks):
        mine, other = both[:count], both[count:]
        all_rows = put(all_rows, place.pair(mine, other, 0), (place.x + k) % place.nx)
    all_rows = all_rows.reshape(length, width)

    out_x = jnp.zeros((place.nx, shard, width), BF16)
    for k in range(place.nx):
        here = out_weight if k == 0 else place.to_x(out_weight, k)
        out_x = put(out_x, here, (place.x - k) % place.nx)
    out_half = gather_dp(place, out_x.reshape(place.nx * shard, width))
    out_half = out_half.reshape(dp * place.nx, 1, shard, width)
    full_out = place.pair(out_half, place.core(out_half), 1).reshape(width, width)

    up_blocks = up_weight.reshape(shard, dp, seq, ff_shard).transpose(2, 0, 1, 3)
    up_block = exchange_seq(place, up_blocks.reshape(seq, shard, hidden_own))
    full_up = gather_dp(place, up_block.reshape(seq * shard, hidden_own))
    full_down = gather_dp(place, down_weight)

    seg_row = segment_ids
    seg_col = segment_ids.reshape(length, 1)
    blocks = length // BLOCK
    ids = segment_ids.reshape(length)
    heads_first = ids[::BLOCK]
    heads_last = ids[BLOCK - 1 :: BLOCK]
    low = jnp.sum(ids[None, :] < heads_first[:, None], axis=1, dtype=jnp.int32)
    high = jnp.sum(ids[None, :] <= heads_last[:, None], axis=1, dtype=jnp.int32)
    bounds = jnp.concatenate([low // BLOCK, (high + BLOCK - 1) // BLOCK])
    own_cols = place.s * head_cols
    query_own = lax.dynamic_slice_in_dim(full_query, own_cols, head_cols, 1)
    value_own = lax.dynamic_slice_in_dim(full_value, own_cols, head_cols, 1)
    qkv_bias = jnp.concatenate([query_own, jnp.zeros_like(query_own), value_own], axis=1)
    qkv = (matmul(all_rows, full_qkv) + qkv_bias).astype(BF16)
    mixed_own, logs = attend(qkv, seg_row, seg_col, bounds, heads)

    mixed = exchange_seq(place, mixed_own.reshape(seq, count, head_cols))
    mixed = mixed.transpose(1, 0, 2).reshape(count, width)
    branch = matmul(mixed, full_out) + bias_out
    first, normed_one, factor_one = norm_forward(rows.astype(F32) + branch, gain_one, shift_one)
    first_low = first.astype(BF16)

    first_all = rows_all(place, first_low)
    hidden_all, slope_all = [], []
    for block in first_all:
        hidden, slope = gelu_pair(matmul(block, full_up) + bias_up)
        hidden_all.append(hidden)
        slope_all.append(slope)
    second = rows_sum(place, [matmul(hidden, full_down) for hidden in hidden_all]) + bias_down
    result, normed_two, factor_two = norm_forward(first + second, gain_two, shift_two)
    output = result.astype(BF16).reshape(tokens.shape)

    grad_out = cotangent.reshape(count, width).astype(F32)
    second_grad, gain_two_grad, shift_two_grad = norm_backward(
        grad_out, normed_two, factor_two, gain_two
    )
    second_low = second_grad.astype(BF16)
    down_bias_grad = jnp.sum(second_low, axis=0, dtype=F32)
    second_all = rows_all(place, second_low)
    preact_all = [
        (right_product(block, full_down) * slope.astype(F32)).astype(BF16)
        for block, slope in zip(second_all, slope_all)
    ]
    first_grad = second_grad + rows_sum(place, [right_product(p, full_up) for p in preact_all])
    down_grad = sum(left_product(h, g) for h, g in zip(hidden_all, second_all))
    up_grad = sum(left_product(f, g) for f, g in zip(first_all, preact_all))
    up_bias_grad = sum(jnp.sum(p, axis=0, dtype=F32) for p in preact_all)
    down_owned = scatter_dp(place, down_grad)
    up_owned = scatter_dp(place, up_grad).astype(BF16)
    up_owned = up_owned.reshape(seq, shard, hidden_own)
    up_owned = exchange_seq(place, up_owned).reshape(seq, shard, dp, ff_shard)
    up_owned = up_owned.transpose(1, 2, 0, 3).reshape(up_weight.shape).astype(F32)

    residual_grad, gain_one_grad, shift_one_grad = norm_backward(
        first_grad, normed_one, factor_one, gain_one
    )
    branch_low = residual_grad.astype(BF16)
    out_bias_grad = jnp.sum(branch_low, axis=0, dtype=F32)
    mixed_grad = right_product(branch_low, full_out).astype(BF16)
    grad_blocks = mixed_grad.reshape(count, seq, head_cols).transpose(1, 0, 2)
    grad_own = exchange_seq(place, grad_blocks).reshape(length, head_cols)

    out_grad = left_product(mixed, branch_low).astype(BF16)
    view = out_grad.reshape(dp * place.nx, CORES, shard, width)
    mine = lax.dynamic_index_in_dim(view, place.c, 1, keepdims=False)
    other = lax.dynamic_index_in_dim(view, 1 - place.c, 1, keepdims=False)
    view = (mine.astype(F32) + place.core(other).astype(F32)).astype(BF16)
    view = view.reshape(dp, place.nx, shard, width)
    summed = lax.dynamic_index_in_dim(view, place.x, 1, keepdims=False).astype(F32)
    for k in range(1, place.nx):
        sent = lax.dynamic_index_in_dim(view, (place.x + k) % place.nx, 1, keepdims=False)
        summed = summed + place.to_x(sent, k).astype(F32)
    out_owned = scatter_dp(place, summed.reshape(dp * shard, width))

    up_bias_wide = lax.dynamic_update_index_in_dim(
        jnp.zeros((dp, seq, ff_shard), F32),
        up_bias_grad.reshape(dp, ff_shard),
        place.s,
        1,
    )
    wide = jnp.concatenate(
        [
            v.reshape(1, width)
            for v in (
                out_bias_grad,
                gain_one_grad,
                shift_one_grad,
                down_bias_grad,
                gain_two_grad,
                shift_two_grad,
            )
        ],
        axis=0,
    ).reshape(6, everyone, shard)
    wide = jnp.concatenate(
        [wide.transpose(1, 0, 2), up_bias_wide.reshape(everyone, ff_shard // shard, shard)], axis=1
    )
    wide = take(all_sum(place, wide), me)
    out_bias_owned, gain_one_owned, shift_one_owned = wide[0], wide[1], wide[2]
    down_bias_owned, gain_two_owned, shift_two_owned = wide[3], wide[4], wide[5]
    up_bias_owned = wide[6:].reshape(ff_shard)

    qkv_grad = attend_back(qkv, mixed_own, grad_own, logs, seg_row, seg_col, bounds, heads)
    joint_grad = left_product(all_rows, qkv_grad)
    joint_owned = scatter_dp(place, joint_grad).astype(BF16)
    joint_owned = exchange_seq(place, joint_owned.reshape(seq, shard, 3 * head_cols))
    joint_owned = joint_owned.reshape(seq, shard, 3, head_cols).transpose(1, 2, 0, 3)
    joint_owned = joint_owned.reshape(qkv_weight.shape).astype(F32)
    sums = jnp.sum(qkv_grad, axis=0, dtype=F32).reshape(3, head_cols)
    ends = jnp.stack([sums[0], sums[2]])[:, None]
    ends = lax.dynamic_update_slice_in_dim(jnp.zeros((2, seq, head_cols), F32), ends, place.s, 1)
    ends = all_sum(place, ends.reshape(2, everyone, shard))
    ends = lax.dynamic_index_in_dim(ends, me, 1, keepdims=False)

    token_parts = right_product(qkv_grad, full_qkv).astype(BF16)
    token_parts = token_parts.reshape(place.nx, CORES, count, width)
    ordered = []
    for k in range(place.nx):
        both = take(token_parts, (place.x + k) % place.nx)
        ordered.append(
            jnp.concatenate([take(both, place.c), take(both, 1 - place.c)], axis=0)
        )
    tokens_grad = (residual_grad + rows_sum(place, ordered)).astype(BF16).reshape(tokens.shape)
    return (
        output,
        tokens_grad,
        joint_owned,
        ends[0],
        ends[1],
        out_owned,
        out_bias_owned,
        gain_one_owned,
        shift_one_owned,
        up_owned,
        up_bias_owned,
        down_owned,
        down_bias_owned,
        gain_two_owned,
        shift_two_owned,
    )


def solution(mesh):
    rows = P("dp", "seq", None)
    matrix = P(("dp", "seq"), None)
    vector = P(("dp", "seq"))
    params = (
        matrix,
        vector,
        vector,
        matrix,
        vector,
        vector,
        vector,
        matrix,
        vector,
        matrix,
        vector,
        vector,
        vector,
    )
    return jax.shard_map(
        partial(body, mesh.shape["dp"], mesh.shape["seq"]),
        mesh=mesh,
        in_specs=(rows, P("dp", None), *params, rows),
        out_specs=(rows, rows, *params),
        check_vma=False,
    )
```

```python
from functools import partial

import jax
import jax.numpy as jnp
from jax import lax
from jax.experimental import pallas as pl
from jax.experimental.pallas import tpu as pltpu
from jax.sharding import PartitionSpec as P

HEADS = 16
HEAD_DIM = 64
EPSILON = 1e-06
MASKED = -1e30
CORES = 2
EXTRA = 16
VMEM = pl.BlockSpec(memory_space=pltpu.VMEM)
F32 = jnp.float32
BF16 = jnp.bfloat16
DN_T = (((1,), (1,)), ((), ()))
DN_L = (((0,), (0,)), ((), ()))


def matmul(left, right):
    return jnp.dot(left, right, preferred_element_type=F32)


def left_product(left, right):
    return lax.dot_general(left, right, DN_L, preferred_element_type=F32)


def right_product(left, right):
    return lax.dot_general(left, right, DN_T, preferred_element_type=F32)


def norm_forward(value, gain, shift):
    mean = jnp.mean(value, axis=-1, keepdims=True)
    centered = value - mean
    variance = jnp.mean(centered * centered, axis=-1, keepdims=True)
    factor = lax.rsqrt(variance + EPSILON)
    normed = centered * factor
    return (normed * gain + shift, normed, factor)


def norm_backward(grad, normed, factor, gain):
    scaled = grad * gain
    inner = jnp.mean(scaled, axis=-1, keepdims=True)
    along = jnp.mean(scaled * normed, axis=-1, keepdims=True)
    return (
        factor * (scaled - inner - normed * along),
        jnp.sum(grad * normed, axis=0),
        jnp.sum(grad, axis=0),
    )


class Place:
    def __init__(self, dp, seq):
        self.dp, self.seq = dp, seq
        self.nx = seq // CORES
        self.ny = min(self.nx, dp)
        self.nz = dp // self.ny
        d = lax.axis_index("dp")
        s = lax.axis_index("seq")
        self.d, self.s = d, s
        self.z, self.y = d // self.ny, d % self.ny
        self.x, self.c = s // CORES, s % CORES

    def core(self, a):
        return lax.ppermute(a, "seq", [(i, i ^ 1) for i in range(self.seq)])

    def to_x(self, a, k):
        n = self.nx
        return lax.ppermute(
            a,
            "seq",
            [(i, ((i // CORES + k) % n) * CORES + i % CORES) for i in range(self.seq)],
        )

    def to_y(self, a, k):
        n = self.ny
        return lax.ppermute(
            a, "dp", [(i, i // n * n + (i % n + k) % n) for i in range(self.dp)]
        )

    def to_z(self, a, k):
        n, m = self.nz, self.ny
        return lax.ppermute(
            a, "dp", [(i, (i // m + k) % n * m + i % m) for i in range(self.dp)]
        )

    def pair(self, own, other, axis):
        first = jnp.where(self.c == 0, own, other)
        second = jnp.where(self.c == 0, other, own)
        return jnp.concatenate([first, second], axis=axis)


def put(buffer, block, index):
    return lax.dynamic_update_slice_in_dim(buffer, block[None], index, 0)


def take(buffer, index):
    return lax.dynamic_index_in_dim(buffer, index, 0, keepdims=False)


def exchange_seq(place, blocks):
    n = place.nx
    view = blocks.reshape(n, CORES, *blocks.shape[1:])
    arrived = []
    for k in range(n):
        send = take(view, (place.x + k) % n)
        arrived.append(place.to_x(send, k) if k else send)
    arrived = jnp.stack(arrived)
    mine = lax.dynamic_index_in_dim(arrived, place.c, 1, keepdims=True)
    other = place.core(lax.dynamic_index_in_dim(arrived, 1 - place.c, 1, keepdims=True))
    both = place.pair(mine, other, 1)
    ordered = jnp.stack([take(both, (place.x - source) % n) for source in range(n)])
    return ordered.reshape(blocks.shape)


def assemble_kernel(plan, counts, where, *refs):
    blocks, outs = refs[: len(plan)], refs[len(plan) :]
    ny, nz = counts
    for block, (k, j, pieces) in zip(blocks, plan):
        owner = lax.rem(where[0] - k + nz, nz) * ny + lax.rem(where[1] - j + ny, ny)
        for i, start, size, col in pieces:
            outs[i][pl.ds(owner, 1), :, col : col + block.shape[1]] = block[start : start + size][None]


class Gather:
    def __init__(self, place, block):
        self.place, self.here, self.k = place, block, 0
        self.blocks = [(0, 0, block)]

    def start(self):
        p = self.place
        self.sent = [p.to_y(self.here, j) for j in range(1, p.ny)]
        self.after = p.to_z(self.here, 1) if self.k < p.nz - 1 else self.here

    def settle(self):
        if self.k == self.place.nz:
            return
        sent, after = lax.optimization_barrier((self.sent, self.after))
        self.blocks += [(self.k, j + 1, b) for j, b in enumerate(sent)]
        self.k += 1
        self.here = after
        if self.k < self.place.nz:
            self.blocks.append((self.k, 0, after))
            self.start()

    def finish(self, pieces, shapes):
        p = self.place
        plan = [(k, j, pieces) for k, j, _ in self.blocks]
        return pl.pallas_call(
            partial(assemble_kernel, plan, (p.ny, p.nz)),
            in_specs=[pl.BlockSpec(memory_space=pltpu.SMEM)] + [VMEM] * len(plan),
            out_specs=[VMEM] * len(shapes),
            out_shape=[jax.ShapeDtypeStruct((p.ny * p.nz, *shape), BF16) for shape in shapes],
            compiler_params=pltpu.CompilerParams(vmem_limit_bytes=32 << 20),
        )(jnp.stack([p.z, p.y]), *[b for _, _, b in self.blocks])


def scatter_dp(place, views, beside):
    ny, nz = place.ny, place.nz

    def piece(z, y):
        return jnp.concatenate(
            [take(v, z * ny + y)[:, c : c + n] for v, c, n in views], axis=0
        )

    total = None
    for k in range(1, nz + 1):
        z = (place.z - k) % nz
        part = piece(z, place.y).astype(F32)
        for j in range(1, ny):
            send = piece(z, (place.y + j) % ny)
            sent = place.to_y(send, j)
            part = part + sent.astype(F32)
        if total is not None:
            send = total.astype(BF16)
            sent = place.to_z(send, 1)
            part = part + sent.astype(F32)
        if k == nz - 1:
            part, _ = lax.optimization_barrier((part, beside))
        total = part
    return total


def pad_rows(values, cols):
    return jnp.pad(values, (0, EXTRA * cols - values.shape[0])).reshape(EXTRA, cols)


def rows_all(place, rows):
    out = []
    for k in range(place.nx):
        here = rows
        if k:
            here = place.to_x(rows, place.nx - k)
        out.append(jnp.concatenate([here, place.core(here)], axis=0))
    return out


def rows_sum(place, part):
    total = None
    for k in reversed(range(place.nx)):
        low = part(k)
        low = low.astype(BF16)
        half = low.shape[0] // 2
        both = low[:half].astype(F32) + place.core(low[half:]).astype(F32)
        if k:
            both = both.astype(BF16)
            both = place.to_x(both, k)
            both = both.astype(F32)
        total = both if total is None else total + both
    return total


BLOCK = 384


def attend_kernel(heads, bounds, qkv_ref, seg_row, seg_col, mixed_ref, log_ref):
    length = qkv_ref.shape[0]
    width = heads * HEAD_DIM
    i = pl.program_id(0)
    start = pl.multiple_of(i * BLOCK, BLOCK)
    cols = pl.ds(start, BLOCK)
    seg_q = seg_row[:, cols]
    queries = [
        qkv_ref[cols, h * HEAD_DIM : (h + 1) * HEAD_DIM] * BF16(HEAD_DIM**-0.5)
        for h in range(heads)
    ]

    def step(j, carry):
        rows = pl.ds(pl.multiple_of(j * BLOCK, BLOCK), BLOCK)
        same = seg_col[rows, :] == seg_q
        out = []
        for h in range(heads):
            high, total, acc = carry[h]
            keys = qkv_ref[rows, width + h * HEAD_DIM : width + (h + 1) * HEAD_DIM]
            values = qkv_ref[rows, 2 * width + h * HEAD_DIM : 2 * width + (h + 1) * HEAD_DIM]
            scores = lax.dot_general(keys, queries[h], DN_T, preferred_element_type=F32)
            scores = jnp.where(same, scores, MASKED)
            new = jnp.maximum(high, jnp.max(scores, axis=0, keepdims=True))
            weights = jnp.exp(scores - new)
            fade = jnp.exp(high - new)
            total = total * fade + jnp.sum(weights, axis=0, keepdims=True)
            acc = acc * fade + lax.dot_general(
                values, weights.astype(BF16), DN_L, preferred_element_type=F32
            )
            out.append((new, total, acc))
        return tuple(out)

    first = tuple(
        (
            jnp.full((1, BLOCK), MASKED, F32),
            jnp.zeros((1, BLOCK), F32),
            jnp.zeros((HEAD_DIM, BLOCK), F32),
        )
        for _ in range(heads)
    )
    done = lax.fori_loop(bounds[i], bounds[i + length // BLOCK], step, first)
    mixed = jnp.concatenate([acc / total for _, total, acc in done], axis=0)
    mixed_ref[...] = mixed.T.astype(BF16)
    log_ref[...] = jnp.concatenate([high + jnp.log(total) for high, total, _ in done], axis=0)


def attend_back_kernel(
    heads, bounds, qkv_ref, mixed_ref, grad_ref, log_ref, seg_row, seg_col, out_ref, acc_ref
):
    length = qkv_ref.shape[0]
    width = heads * HEAD_DIM
    scale = HEAD_DIM**-0.5
    i = pl.program_id(0)

    @pl.when(i == 0)
    def _():
        acc_ref[...] = jnp.zeros_like(acc_ref)

    start = pl.multiple_of(i * BLOCK, BLOCK)
    cols = pl.ds(start, BLOCK)
    seg_q = seg_row[:, cols]
    grads_all = grad_ref[cols, :]
    along = (grads_all.astype(F32) * mixed_ref[cols, :].astype(F32)).T
    along = [
        jnp.sum(along[h * HEAD_DIM : (h + 1) * HEAD_DIM], axis=0, keepdims=True)
        for h in range(heads)
    ]
    logs = [log_ref[h : h + 1, cols] for h in range(heads)]
    queries = [
        qkv_ref[cols, h * HEAD_DIM : (h + 1) * HEAD_DIM] * BF16(scale) for h in range(heads)
    ]
    grads = [grads_all[:, h * HEAD_DIM : (h + 1) * HEAD_DIM] for h in range(heads)]

    def step(j, carry):
        rows = pl.ds(pl.multiple_of(j * BLOCK, BLOCK), BLOCK)
        same = seg_col[rows, :] == seg_q
        out, key_parts, value_parts = [], [], []
        for h in range(heads):
            keys = qkv_ref[rows, width + h * HEAD_DIM : width + (h + 1) * HEAD_DIM]
            values = qkv_ref[rows, 2 * width + h * HEAD_DIM : 2 * width + (h + 1) * HEAD_DIM]
            scores = lax.dot_general(keys, queries[h], DN_T, preferred_element_type=F32)
            shares = jnp.exp(jnp.where(same, scores, MASKED) - logs[h])
            shares_grad = lax.dot_general(values, grads[h], DN_T, preferred_element_type=F32)
            score_low = (shares * (shares_grad - along[h])).astype(BF16)
            value_parts.append(matmul(shares.astype(BF16), grads[h]))
            key_parts.append(matmul(score_low, queries[h]))
            out.append(
                carry[h] + lax.dot_general(keys, score_low, DN_L, preferred_element_type=F32)
            )
        acc_ref[rows, :width] += jnp.concatenate(key_parts, axis=1)
        acc_ref[rows, width:] += jnp.concatenate(value_parts, axis=1)
        return tuple(out)

    first = tuple(jnp.zeros((HEAD_DIM, BLOCK), F32) for _ in range(heads))
    done = lax.fori_loop(bounds[i], bounds[i + length // BLOCK], step, first)
    out_ref[cols, :width] = (jnp.concatenate(done, axis=0) * scale).T.astype(BF16)

    @pl.when(i == length // BLOCK - 1)
    def _():
        out_ref[:, width:] = acc_ref[...].astype(BF16)


def attend(qkv, seg_row, seg_col, bounds, heads):
    length = qkv.shape[0]
    width = heads * HEAD_DIM
    return pl.pallas_call(
        partial(attend_kernel, heads),
        grid_spec=pltpu.PrefetchScalarGridSpec(
            num_scalar_prefetch=1,
            grid=(length // BLOCK,),
            in_specs=[VMEM, VMEM, VMEM],
            out_specs=[
                pl.BlockSpec((BLOCK, width), lambda i, b: (i, 0)),
                pl.BlockSpec((heads, BLOCK), lambda i, b: (0, i)),
            ],
        ),
        out_shape=[
            jax.ShapeDtypeStruct((length, width), BF16),
            jax.ShapeDtypeStruct((heads, length), F32),
        ],
        compiler_params=pltpu.CompilerParams(vmem_limit_bytes=40 << 20),
        cost_estimate=pl.CostEstimate(
            flops=4 * length * length * width,
            bytes_accessed=8 * length * width,
            transcendentals=length * length * heads,
        ),
    )(bounds, qkv, seg_row, seg_col)


def attend_back(qkv, mixed, grad, logs, seg_row, seg_col, bounds, heads):
    length = qkv.shape[0]
    width = heads * HEAD_DIM
    return pl.pallas_call(
        partial(attend_back_kernel, heads),
        grid_spec=pltpu.PrefetchScalarGridSpec(
            num_scalar_prefetch=1,
            grid=(length // BLOCK,),
            in_specs=[VMEM] * 6,
            out_specs=VMEM,
            scratch_shapes=[pltpu.VMEM((length, 2 * width), F32)],
        ),
        out_shape=jax.ShapeDtypeStruct((length, 3 * width), BF16),
        compiler_params=pltpu.CompilerParams(vmem_limit_bytes=40 << 20),
        cost_estimate=pl.CostEstimate(
            flops=10 * length * length * width,
            bytes_accessed=16 * length * width,
            transcendentals=length * length * heads,
        ),
    )(bounds, qkv, mixed, grad, logs, seg_row, seg_col)


TILE = 256


def grads_kernel(count, *refs):
    out_ref = refs[-1]
    out_ref[...] = sum(left_product(refs[i][...], refs[count + i][...]) for i in range(count)).astype(
        BF16
    )


def weight_grads(lefts, rights):
    count = len(lefts)
    inner, cols = lefts[0].shape[1], rights[0].shape[1]
    tile = min(TILE, inner)
    return pl.pallas_call(
        partial(grads_kernel, count),
        grid=(inner // tile,),
        in_specs=[pl.BlockSpec((v.shape[0], tile), lambda i: (0, i)) for v in lefts]
        + [pl.BlockSpec(v.shape, lambda i: (0, 0)) for v in rights],
        out_specs=pl.BlockSpec((tile, cols), lambda i: (i, 0)),
        out_shape=jax.ShapeDtypeStruct((inner, cols), BF16),
        compiler_params=pltpu.CompilerParams(vmem_limit_bytes=40 << 20),
        cost_estimate=pl.CostEstimate(
            flops=2 * sum(v.shape[0] for v in lefts) * inner * cols,
            bytes_accessed=2 * sum(v.size for v in (*lefts, *rights)) + 2 * inner * cols,
            transcendentals=0,
        ),
    )(*lefts, *rights)


def gelu_pair(preact):
    half = 0.5 + 0.5 * lax.erf(preact * (2.0**-0.5))
    slope = half + preact * jnp.exp(-0.5 * preact * preact) * 0.3989422804014327
    return (preact * half).astype(BF16), slope.astype(BF16)


def body(
    dp,
    seq,
    tokens,
    segment_ids,
    qkv_weight,
    query_bias,
    value_bias,
    out_weight,
    out_bias,
    first_gain,
    first_shift,
    up_weight,
    up_bias,
    down_weight,
    down_bias,
    second_gain,
    second_shift,
    cotangent,
):
    place = Place(dp, seq)
    everyone = dp * seq
    _, count, width = tokens.shape
    hidden_own = up_weight.shape[1] // seq
    heads = HEADS // seq
    head_cols = heads * HEAD_DIM
    shard = qkv_weight.shape[0]
    ff_shard = down_weight.shape[0]
    length = segment_ids.shape[1]
    rows = tokens.reshape(count, width)

    qkv_cols = 3 * head_cols
    smalls = (query_bias, value_bias, out_bias, first_gain, first_shift, down_bias, second_gain, second_shift)
    packed = jnp.concatenate([*smalls, up_bias])
    qkv_blocks = qkv_weight.reshape(shard, 3, seq, head_cols).transpose(2, 0, 1, 3)
    up_blocks = up_weight.reshape(shard, dp, seq, ff_shard).transpose(2, 0, 1, 3)
    blocks = jnp.concatenate(
        [qkv_blocks.reshape(seq, shard, qkv_cols), up_blocks.reshape(seq, shard, hidden_own)], axis=2
    )
    extra = jnp.broadcast_to(pad_rows(packed, blocks.shape[2]), (seq, EXTRA, blocks.shape[2]))
    blocks = exchange_seq(place, jnp.concatenate([blocks, extra], axis=1))
    qkv_block = blocks[:, :shard, :qkv_cols].reshape(seq * shard, qkv_cols)
    up_block = blocks[:, :shard, qkv_cols:].reshape(seq * shard, hidden_own)
    packed_seq = blocks[:, shard, : packed.shape[0]].reshape(-1)
    out_x = jnp.zeros((place.nx, shard, width), BF16)
    for k in range(place.nx):
        here = out_weight if k == 0 else place.to_x(out_weight, k)
        out_x = put(out_x, here, (place.x - k) % place.nx)
    out_x = out_x.reshape(place.nx * shard, width)

    def columns(a):
        return [a[:, i : i + head_cols] for i in range(0, a.shape[1], head_cols)]

    stack = [(0, b, i * head_cols) for i, b in enumerate(columns(qkv_block))]
    stack += [(1, b, i * head_cols) for i, b in enumerate(columns(out_x))]
    stack += [(2, pad_rows(packed_seq, head_cols), 0)]
    pieces, at = [], 0
    for i, b, col in stack:
        pieces.append((i, at, b.shape[0], col))
        at += b.shape[0]
    attention = Gather(place, jnp.concatenate([b for _, b, _ in stack], axis=0))
    attention.start()
    for _ in range(place.nz - 1):
        attention.settle()
    up_block, down_late, _ = lax.optimization_barrier((up_block, down_weight, attention.here))
    full_up = lax.all_gather(up_block, "dp", axis=0, tiled=True)
    full_down = lax.all_gather(down_late, "dp", axis=0, tiled=True)
    attention.settle()
    full_qkv, packed_all = attention.finish(
        [(i // 2, *rest) for i, *rest in pieces if i != 1], ((seq * shard, qkv_cols), (EXTRA, head_cols))
    )
    (out_half,) = attention.finish(
        [(0, *rest) for i, *rest in pieces if i == 1], ((place.nx * shard, width),)
    )
    out_half = out_half.reshape(dp * place.nx, 1, shard, width)
    full_out = place.pair(out_half, place.core(out_half), 1).reshape(width, width)
    full_qkv = full_qkv.reshape(width, qkv_cols)
    packed_all = packed_all.reshape(dp, -1)[:, : packed_seq.shape[0]]
    packed_all = packed_all.reshape(dp, seq, packed.shape[0]).astype(F32)
    vectors = [
        packed_all[:, :, i * shard : (i + 1) * shard].reshape(1, width) for i in range(len(smalls))
    ]
    full_query, full_value, bias_out, gain_one, shift_one, bias_down, gain_two, shift_two = vectors
    bias_up = lax.dynamic_index_in_dim(packed_all, place.s, 1, keepdims=False)
    bias_up = bias_up[:, len(smalls) * shard :].reshape(1, hidden_own)

    row_blocks = rows_all(place, rows)
    all_rows = jnp.zeros((place.nx, CORES * count, width), BF16)
    for k, both in enumerate(row_blocks):
        mine, other = both[:count], both[count:]
        all_rows = put(all_rows, place.pair(mine, other, 0), (place.x + k) % place.nx)
    all_rows = all_rows.reshape(length, width)

    seg_row = segment_ids
    seg_col = segment_ids.reshape(length, 1)
    blocks = length // BLOCK
    ids = segment_ids.reshape(length)
    heads_first = ids[::BLOCK]
    heads_last = ids[BLOCK - 1 :: BLOCK]
    low = jnp.sum(ids[None, :] < heads_first[:, None], axis=1, dtype=jnp.int32)
    high = jnp.sum(ids[None, :] <= heads_last[:, None], axis=1, dtype=jnp.int32)
    bounds = jnp.concatenate([low // BLOCK, (high + BLOCK - 1) // BLOCK])
    own_cols = place.s * head_cols
    query_own = lax.dynamic_slice_in_dim(full_query, own_cols, head_cols, 1)
    value_own = lax.dynamic_slice_in_dim(full_value, own_cols, head_cols, 1)
    qkv_bias = jnp.concatenate([query_own, jnp.zeros_like(query_own), value_own], axis=1)
    qkv = (matmul(all_rows, full_qkv) + qkv_bias).astype(BF16)
    mixed_own, logs = attend(qkv, seg_row, seg_col, bounds, heads)

    mixed = exchange_seq(place, mixed_own.reshape(seq, count, head_cols))
    mixed = mixed.transpose(1, 0, 2).reshape(count, width)
    branch = matmul(mixed, full_out) + bias_out
    first, normed_one, factor_one = norm_forward(rows.astype(F32) + branch, gain_one, shift_one)
    first_low = first.astype(BF16)
    first_all = rows_all(place, first_low)
    hidden_all, slope_all = [], []
    for k, block in enumerate(first_all):
        preact = matmul(block, full_up)
        hidden, slope = gelu_pair(preact + bias_up)
        hidden_all.append(hidden)
        slope_all.append(slope)
    second = rows_sum(place, lambda k: matmul(hidden_all[k], full_down)) + bias_down
    result, normed_two, factor_two = norm_forward(first + second, gain_two, shift_two)
    output = result.astype(BF16).reshape(tokens.shape)

    grad_out = cotangent.reshape(count, width).astype(F32)
    second_grad, gain_two_grad, shift_two_grad = norm_backward(
        grad_out, normed_two, factor_two, gain_two
    )
    second_low = second_grad.astype(BF16)
    down_bias_grad = jnp.sum(second_low, axis=0, dtype=F32)
    second_all = rows_all(place, second_low)
    preact_all = []
    for k, (block, slope) in enumerate(zip(second_all, slope_all)):
        hidden_grad = right_product(block, full_down)
        preact_all.append((hidden_grad * slope.astype(F32)).astype(BF16))
    first_grad = second_grad + rows_sum(place, lambda k: right_product(preact_all[k], full_up))
    down_grad = weight_grads(hidden_all, second_all)
    down_owned = lax.psum_scatter(down_grad, "dp", scatter_dimension=0, tiled=True).astype(F32)
    up_grad = weight_grads(first_all, preact_all)
    up_owned = lax.psum_scatter(up_grad, "dp", scatter_dimension=0, tiled=True)
    up_bias_grad = sum(jnp.sum(p, axis=0, dtype=F32) for p in preact_all)

    residual_grad, gain_one_grad, shift_one_grad = norm_backward(
        first_grad, normed_one, factor_one, gain_one
    )
    branch_low = residual_grad.astype(BF16)
    out_bias_grad = jnp.sum(branch_low, axis=0, dtype=F32)
    mixed_grad = right_product(branch_low, full_out).astype(BF16)
    grad_blocks = mixed_grad.reshape(count, seq, head_cols).transpose(1, 0, 2)
    grad_own = exchange_seq(place, grad_blocks).reshape(length, head_cols)

    up_bias_wide = lax.dynamic_update_index_in_dim(
        jnp.zeros((dp, seq, ff_shard), F32), up_bias_grad.reshape(dp, ff_shard), place.s, 1
    ).reshape(everyone, ff_shard)
    vector_sums = (
        out_bias_grad,
        gain_one_grad,
        shift_one_grad,
        down_bias_grad,
        gain_two_grad,
        shift_two_grad,
    )
    extra = jnp.concatenate([v.reshape(everyone, shard) for v in vector_sums] + [up_bias_wide], axis=1)
    wide_count = extra.shape[1]
    extra = jnp.pad(extra.astype(BF16)[:, None], ((0, 0), (0, EXTRA - 1), (0, width - wide_count)))
    out_grad = weight_grads([mixed], [branch_low]).reshape(everyone, shard, width)
    view = jnp.concatenate([out_grad, extra], axis=1)
    view = view.reshape(dp * place.nx, CORES, shard + EXTRA, width)
    mine = lax.dynamic_index_in_dim(view, place.c, 1, keepdims=False)
    other = lax.dynamic_index_in_dim(view, 1 - place.c, 1, keepdims=False)
    view = (mine.astype(F32) + place.core(other).astype(F32)).astype(BF16)
    view = view.reshape(dp, place.nx, shard + EXTRA, width)
    summed = lax.dynamic_index_in_dim(view, place.x, 1, keepdims=False).astype(F32)
    for k in range(1, place.nx):
        sent = lax.dynamic_index_in_dim(view, (place.x + k) % place.nx, 1, keepdims=False)
        summed = summed + place.to_x(sent, k).astype(F32)
    qkv_grad = attend_back(qkv, mixed_own, grad_own, logs, seg_row, seg_col, bounds, heads)
    qkv_grad, summed = lax.optimization_barrier((qkv_grad, summed))
    token_parts = right_product(qkv_grad, full_qkv).astype(BF16)
    token_parts = token_parts.reshape(place.nx, CORES, count, width)
    ordered = []
    for k in range(place.nx):
        both = take(token_parts, (place.x + k) % place.nx)
        ordered.append(
            jnp.concatenate([take(both, place.c), take(both, 1 - place.c)], axis=0)
        )
    token_sum = rows_sum(place, lambda k: ordered[k])
    joint_grad = weight_grads([all_rows], [qkv_grad])
    up_owned = up_owned.reshape(seq, shard, hidden_own)
    up_owned = exchange_seq(place, up_owned).reshape(seq, shard, dp, ff_shard)
    up_owned = up_owned.transpose(1, 2, 0, 3).reshape(up_weight.shape).astype(F32)

    joint_grad = joint_grad.reshape(dp, seq * shard, qkv_cols)
    sums = jnp.sum(qkv_grad, axis=0, dtype=F32).reshape(3, head_cols)
    ends = jnp.stack([sums[0], sums[2]])
    ends = lax.dynamic_update_slice_in_dim(jnp.zeros((2, width), F32), ends, own_cols, 1)
    ends = ends.reshape(2, dp, seq * shard).transpose(1, 0, 2).reshape(dp, 1, 2 * seq * shard)
    ends = jnp.pad(ends.astype(BF16), ((0, 0), (0, EXTRA - 1), (0, head_cols - 2 * seq * shard)))
    views = [(joint_grad, i * head_cols, head_cols) for i in range(3)]
    views += [(ends, 0, head_cols)]
    views += [(summed.astype(BF16), i, head_cols) for i in range(0, width, head_cols)]
    owned = scatter_dp(place, views, token_sum)
    per = seq * shard
    joint = jnp.concatenate([owned[i * per : (i + 1) * per] for i in range(3)], axis=1).astype(BF16)
    ends = owned[3 * per]
    owned = owned[3 * per + EXTRA :].reshape(-1, shard + EXTRA, head_cols)
    out_owned = owned[:, :shard].transpose(1, 0, 2).reshape(shard, width)
    wide = owned[:, shard].reshape(width)
    out_bias_owned, gain_one_owned, shift_one_owned, down_bias_owned, gain_two_owned, shift_two_owned = [
        wide[i * shard : (i + 1) * shard] for i in range(len(vector_sums))
    ]
    up_bias_owned = wide[len(vector_sums) * shard : wide_count]
    ends = ends[: 2 * per].astype(BF16).reshape(2, seq, shard).transpose(1, 0, 2)
    ends = jnp.pad(
        ends.reshape(seq, 1, 2 * shard), ((0, 0), (0, EXTRA - 1), (0, qkv_cols - 2 * shard))
    )
    joint = jnp.concatenate([joint.reshape(seq, shard, qkv_cols), ends], axis=1)
    joint = exchange_seq(place, joint)
    joint_owned = joint[:, :shard].reshape(seq, shard, 3, head_cols).transpose(1, 2, 0, 3)
    joint_owned = joint_owned.reshape(qkv_weight.shape).astype(F32)
    ends = jnp.sum(joint[:, shard, : 2 * shard].astype(F32), axis=0).reshape(2, shard)

    tokens_grad = (residual_grad + token_sum).astype(BF16).reshape(tokens.shape)
    return (
        output,
        tokens_grad,
        joint_owned,
        ends[0],
        ends[1],
        out_owned,
        out_bias_owned,
        gain_one_owned,
        shift_one_owned,
        up_owned,
        up_bias_owned,
        down_owned,
        down_bias_owned,
        gain_two_owned,
        shift_two_owned,
    )


def solution(mesh):
    rows = P("dp", "seq", None)
    matrix = P(("dp", "seq"), None)
    vector = P(("dp", "seq"))
    params = (
        matrix,
        vector,
        vector,
        matrix,
        vector,
        vector,
        vector,
        matrix,
        vector,
        matrix,
        vector,
        vector,
        vector,
    )
    return jax.shard_map(
        partial(body, mesh.shape["dp"], mesh.shape["seq"]),
        mesh=mesh,
        in_specs=(rows, P("dp", None), *params, rows),
        out_specs=(rows, rows, *params),
        check_vma=False,
    )
```

```python
from functools import partial

import jax
import jax.numpy as jnp
from jax import lax
from jax.experimental import pallas as pl
from jax.experimental.pallas import tpu as pltpu
from jax.sharding import PartitionSpec as P

HEADS = 16
HEAD_DIM = 64
EPSILON = 1e-06
MASKED = -1e30
CORES = 2
EXTRA = 16
VMEM = pl.BlockSpec(memory_space=pltpu.VMEM)
F32 = jnp.float32
BF16 = jnp.bfloat16
DN_T = (((1,), (1,)), ((), ()))
DN_L = (((0,), (0,)), ((), ()))


def matmul(left, right):
    return jnp.dot(left, right, preferred_element_type=F32)


def left_product(left, right):
    return lax.dot_general(left, right, DN_L, preferred_element_type=F32)


def right_product(left, right):
    return lax.dot_general(left, right, DN_T, preferred_element_type=F32)


def norm_forward(value, gain, shift):
    mean = jnp.mean(value, axis=-1, keepdims=True)
    centered = value - mean
    variance = jnp.mean(centered * centered, axis=-1, keepdims=True)
    factor = lax.rsqrt(variance + EPSILON)
    normed = centered * factor
    return (normed * gain + shift, normed, factor)


def norm_backward(grad, normed, factor, gain):
    scaled = grad * gain
    inner = jnp.mean(scaled, axis=-1, keepdims=True)
    along = jnp.mean(scaled * normed, axis=-1, keepdims=True)
    return (
        factor * (scaled - inner - normed * along),
        jnp.sum(grad * normed, axis=0),
        jnp.sum(grad, axis=0),
    )


class Place:
    def __init__(self, dp, seq):
        self.dp, self.seq = dp, seq
        self.nx = seq // CORES
        self.ny = min(self.nx, dp)
        self.nz = dp // self.ny
        d = lax.axis_index("dp")
        s = lax.axis_index("seq")
        self.d, self.s = d, s
        self.z, self.y = d // self.ny, d % self.ny
        self.x, self.c = s // CORES, s % CORES

    def core(self, a):
        return lax.ppermute(a, "seq", [(i, i ^ 1) for i in range(self.seq)])

    def to_x(self, a, k):
        n = self.nx
        return lax.ppermute(
            a,
            "seq",
            [(i, ((i // CORES + k) % n) * CORES + i % CORES) for i in range(self.seq)],
        )

    def to_y(self, a, k):
        n = self.ny
        return lax.ppermute(
            a, "dp", [(i, i // n * n + (i % n + k) % n) for i in range(self.dp)]
        )

    def to_z(self, a, k):
        n, m = self.nz, self.ny
        return lax.ppermute(
            a, "dp", [(i, (i // m + k) % n * m + i % m) for i in range(self.dp)]
        )

    def pair(self, own, other, axis):
        first = jnp.where(self.c == 0, own, other)
        second = jnp.where(self.c == 0, other, own)
        return jnp.concatenate([first, second], axis=axis)


def put(buffer, block, index):
    return lax.dynamic_update_slice_in_dim(buffer, block[None], index, 0)


def take(buffer, index):
    return lax.dynamic_index_in_dim(buffer, index, 0, keepdims=False)


def exchange_seq(place, blocks):
    n = place.nx
    view = blocks.reshape(n, CORES, *blocks.shape[1:])
    arrived = []
    for k in range(n):
        send = take(view, (place.x + k) % n)
        arrived.append(place.to_x(send, k) if k else send)
    arrived = jnp.stack(arrived)
    mine = lax.dynamic_index_in_dim(arrived, place.c, 1, keepdims=True)
    other = place.core(lax.dynamic_index_in_dim(arrived, 1 - place.c, 1, keepdims=True))
    both = place.pair(mine, other, 1)
    ordered = jnp.stack([take(both, (place.x - source) % n) for source in range(n)])
    return ordered.reshape(blocks.shape)


def assemble_kernel(plan, counts, where, *refs):
    blocks, outs = refs[: len(plan)], refs[len(plan) :]
    ny, nz = counts
    for block, (k, j, pieces) in zip(blocks, plan):
        owner = lax.rem(where[0] - k + nz, nz) * ny + lax.rem(where[1] - j + ny, ny)
        for i, start, size, col in pieces:
            outs[i][pl.ds(owner, 1), :, col : col + block.shape[1]] = block[start : start + size][None]


class Gather:
    def __init__(self, place, block):
        self.place, self.here, self.k = place, block, 0
        self.blocks = [(0, 0, block)]

    def start(self):
        p = self.place
        self.sent = [p.to_y(self.here, j) for j in range(1, p.ny)]
        self.after = p.to_z(self.here, 1) if self.k < p.nz - 1 else self.here

    def settle(self):
        if self.k == self.place.nz:
            return
        sent, after = lax.optimization_barrier((self.sent, self.after))
        self.blocks += [(self.k, j + 1, b) for j, b in enumerate(sent)]
        self.k += 1
        self.here = after
        if self.k < self.place.nz:
            self.blocks.append((self.k, 0, after))
            self.start()

    def finish(self, pieces, shapes):
        p = self.place
        plan = [(k, j, pieces) for k, j, _ in self.blocks]
        return pl.pallas_call(
            partial(assemble_kernel, plan, (p.ny, p.nz)),
            in_specs=[pl.BlockSpec(memory_space=pltpu.SMEM)] + [VMEM] * len(plan),
            out_specs=[VMEM] * len(shapes),
            out_shape=[jax.ShapeDtypeStruct((p.ny * p.nz, *shape), BF16) for shape in shapes],
            compiler_params=pltpu.CompilerParams(vmem_limit_bytes=32 << 20),
        )(jnp.stack([p.z, p.y]), *[b for _, _, b in self.blocks])


def scatter_dp(place, views, beside):
    ny, nz = place.ny, place.nz

    def piece(z, y):
        return jnp.concatenate(
            [take(v, z * ny + y)[:, c : c + n] for v, c, n in views], axis=0
        )

    total = None
    for k in range(1, nz + 1):
        z = (place.z - k) % nz
        part = piece(z, place.y).astype(F32)
        for j in range(1, ny):
            send = piece(z, (place.y + j) % ny)
            sent = place.to_y(send, j)
            part = part + sent.astype(F32)
        if total is not None:
            send = total.astype(BF16)
            sent = place.to_z(send, 1)
            part = part + sent.astype(F32)
        if k == nz - 1:
            part, _ = lax.optimization_barrier((part, beside))
        total = part
    return total


def rows_each(place, rows, work):
    sent = [place.to_x(rows, place.nx - k) for k in range(1, place.nx)]
    blocks, done = [], []
    for k in range(place.nx):
        here = rows
        if k:
            here, _ = lax.optimization_barrier((sent[k - 1], done[-1]))
        blocks.append(jnp.concatenate([here, place.core(here)], axis=0))
        done.append(work(k, blocks[-1]))
    return blocks, done


def rows_sum(place, values, part):
    total, both = None, None
    for k in reversed(range(place.nx)):
        value = values[k]
        if both is not None:
            value, _ = lax.optimization_barrier((value, both))
        low = part(value).astype(BF16)
        half = low.shape[0] // 2
        both = low[:half].astype(F32) + place.core(low[half:]).astype(F32)
        term = both
        if k:
            both = both.astype(BF16)
            term = place.to_x(both, k).astype(F32)
        total = term if total is None else total + term
    return total


BLOCK = 384


def attend_kernel(heads, bounds, qkv_ref, seg_row, seg_col, mixed_ref, log_ref):
    length = qkv_ref.shape[0]
    width = heads * HEAD_DIM
    i = pl.program_id(0)
    start = pl.multiple_of(i * BLOCK, BLOCK)
    cols = pl.ds(start, BLOCK)
    seg_q = seg_row[:, cols]
    queries = [
        qkv_ref[cols, h * HEAD_DIM : (h + 1) * HEAD_DIM] * BF16(HEAD_DIM**-0.5)
        for h in range(heads)
    ]

    def step(j, carry):
        rows = pl.ds(pl.multiple_of(j * BLOCK, BLOCK), BLOCK)
        same = seg_col[rows, :] == seg_q
        out = []
        for h in range(heads):
            high, total, acc = carry[h]
            keys = qkv_ref[rows, width + h * HEAD_DIM : width + (h + 1) * HEAD_DIM]
            values = qkv_ref[rows, 2 * width + h * HEAD_DIM : 2 * width + (h + 1) * HEAD_DIM]
            scores = lax.dot_general(keys, queries[h], DN_T, preferred_element_type=F32)
            scores = jnp.where(same, scores, MASKED)
            new = jnp.maximum(high, jnp.max(scores, axis=0, keepdims=True))
            weights = jnp.exp(scores - new)
            fade = jnp.exp(high - new)
            total = total * fade + jnp.sum(weights, axis=0, keepdims=True)
            acc = acc * fade + lax.dot_general(
                values, weights.astype(BF16), DN_L, preferred_element_type=F32
            )
            out.append((new, total, acc))
        return tuple(out)

    first = tuple(
        (
            jnp.full((1, BLOCK), MASKED, F32),
            jnp.zeros((1, BLOCK), F32),
            jnp.zeros((HEAD_DIM, BLOCK), F32),
        )
        for _ in range(heads)
    )
    done = lax.fori_loop(bounds[i], bounds[i + length // BLOCK], step, first)
    mixed = jnp.concatenate([acc / total for _, total, acc in done], axis=0)
    mixed_ref[...] = mixed.T.astype(BF16)
    log_ref[...] = jnp.concatenate([high + jnp.log(total) for high, total, _ in done], axis=0)


def attend_back_kernel(
    heads, bounds, qkv_ref, mixed_ref, grad_ref, log_ref, seg_row, seg_col, out_ref, acc_ref
):
    length = qkv_ref.shape[0]
    width = heads * HEAD_DIM
    scale = HEAD_DIM**-0.5
    i = pl.program_id(0)

    @pl.when(i == 0)
    def _():
        acc_ref[...] = jnp.zeros_like(acc_ref)

    start = pl.multiple_of(i * BLOCK, BLOCK)
    cols = pl.ds(start, BLOCK)
    seg_q = seg_row[:, cols]
    grads_all = grad_ref[cols, :]
    along = (grads_all.astype(F32) * mixed_ref[cols, :].astype(F32)).T
    along = [
        jnp.sum(along[h * HEAD_DIM : (h + 1) * HEAD_DIM], axis=0, keepdims=True)
        for h in range(heads)
    ]
    logs = [log_ref[h : h + 1, cols] for h in range(heads)]
    queries = [
        qkv_ref[cols, h * HEAD_DIM : (h + 1) * HEAD_DIM] * BF16(scale) for h in range(heads)
    ]
    grads = [grads_all[:, h * HEAD_DIM : (h + 1) * HEAD_DIM] for h in range(heads)]

    def step(j, carry):
        rows = pl.ds(pl.multiple_of(j * BLOCK, BLOCK), BLOCK)
        same = seg_col[rows, :] == seg_q
        out, key_parts, value_parts = [], [], []
        for h in range(heads):
            keys = qkv_ref[rows, width + h * HEAD_DIM : width + (h + 1) * HEAD_DIM]
            values = qkv_ref[rows, 2 * width + h * HEAD_DIM : 2 * width + (h + 1) * HEAD_DIM]
            scores = lax.dot_general(keys, queries[h], DN_T, preferred_element_type=F32)
            shares = jnp.exp(jnp.where(same, scores, MASKED) - logs[h])
            shares_grad = lax.dot_general(values, grads[h], DN_T, preferred_element_type=F32)
            score_low = (shares * (shares_grad - along[h])).astype(BF16)
            value_parts.append(matmul(shares.astype(BF16), grads[h]))
            key_parts.append(matmul(score_low, queries[h]))
            out.append(
                carry[h] + lax.dot_general(keys, score_low, DN_L, preferred_element_type=F32)
            )
        acc_ref[rows, :width] += jnp.concatenate(key_parts, axis=1)
        acc_ref[rows, width:] += jnp.concatenate(value_parts, axis=1)
        return tuple(out)

    first = tuple(jnp.zeros((HEAD_DIM, BLOCK), F32) for _ in range(heads))
    done = lax.fori_loop(bounds[i], bounds[i + length // BLOCK], step, first)
    out_ref[cols, :width] = (jnp.concatenate(done, axis=0) * scale).T.astype(BF16)

    @pl.when(i == length // BLOCK - 1)
    def _():
        out_ref[:, width:] = acc_ref[...].astype(BF16)


def attend(qkv, seg_row, seg_col, bounds, heads):
    length = qkv.shape[0]
    width = heads * HEAD_DIM
    return pl.pallas_call(
        partial(attend_kernel, heads),
        grid_spec=pltpu.PrefetchScalarGridSpec(
            num_scalar_prefetch=1,
            grid=(length // BLOCK,),
            in_specs=[VMEM, VMEM, VMEM],
            out_specs=[
                pl.BlockSpec((BLOCK, width), lambda i, b: (i, 0)),
                pl.BlockSpec((heads, BLOCK), lambda i, b: (0, i)),
            ],
        ),
        out_shape=[
            jax.ShapeDtypeStruct((length, width), BF16),
            jax.ShapeDtypeStruct((heads, length), F32),
        ],
        compiler_params=pltpu.CompilerParams(vmem_limit_bytes=40 << 20),
        cost_estimate=pl.CostEstimate(
            flops=4 * length * length * width,
            bytes_accessed=8 * length * width,
            transcendentals=length * length * heads,
        ),
    )(bounds, qkv, seg_row, seg_col)


def attend_back(qkv, mixed, grad, logs, seg_row, seg_col, bounds, heads):
    length = qkv.shape[0]
    width = heads * HEAD_DIM
    return pl.pallas_call(
        partial(attend_back_kernel, heads),
        grid_spec=pltpu.PrefetchScalarGridSpec(
            num_scalar_prefetch=1,
            grid=(length // BLOCK,),
            in_specs=[VMEM] * 6,
            out_specs=VMEM,
            scratch_shapes=[pltpu.VMEM((length, 2 * width), F32)],
        ),
        out_shape=jax.ShapeDtypeStruct((length, 3 * width), BF16),
        compiler_params=pltpu.CompilerParams(vmem_limit_bytes=40 << 20),
        cost_estimate=pl.CostEstimate(
            flops=10 * length * length * width,
            bytes_accessed=16 * length * width,
            transcendentals=length * length * heads,
        ),
    )(bounds, qkv, mixed, grad, logs, seg_row, seg_col)


TILE = 256


def grads_kernel(count, *refs):
    out_ref = refs[-1]
    at = 0
    for i in range(0, len(refs) - 1, 2 * count):
        lefts, rights = refs[i : i + count], refs[i + count : i + 2 * count]
        cols = rights[0].shape[1]
        total = sum(left_product(a[...], b[...]) for a, b in zip(lefts, rights))
        out_ref[:, at : at + cols] = total.astype(BF16)
        at += cols


def weight_grads(*sides):
    count = len(sides[0])
    inner = sides[0][0].shape[1]
    cols = sum(rights[0].shape[1] for rights in sides[1::2])
    tile = min(TILE, inner)
    specs, values = [], []
    for n, side in enumerate(sides):
        for v in side:
            values.append(v)
            if n % 2:
                specs.append(VMEM)
            else:
                specs.append(pl.BlockSpec((v.shape[0], tile), lambda i: (0, i)))
    rows = sum(v.shape[0] for v in sides[0])
    return pl.pallas_call(
        partial(grads_kernel, count),
        grid=(inner // tile,),
        in_specs=specs,
        out_specs=pl.BlockSpec((tile, cols), lambda i: (i, 0)),
        out_shape=jax.ShapeDtypeStruct((inner, cols), BF16),
        compiler_params=pltpu.CompilerParams(vmem_limit_bytes=40 << 20),
        cost_estimate=pl.CostEstimate(
            flops=2 * rows * inner * cols,
            bytes_accessed=2 * sum(v.size for v in values) + 2 * inner * cols,
            transcendentals=0,
        ),
    )(*values)


def gelu_pair(preact):
    half = 0.5 + 0.5 * lax.erf(preact * (2.0**-0.5))
    slope = half + preact * jnp.exp(-0.5 * preact * preact) * 0.3989422804014327
    return (preact * half).astype(BF16), slope.astype(BF16)


def body(
    dp,
    seq,
    tokens,
    segment_ids,
    qkv_weight,
    query_bias,
    value_bias,
    out_weight,
    out_bias,
    first_gain,
    first_shift,
    up_weight,
    up_bias,
    down_weight,
    down_bias,
    second_gain,
    second_shift,
    cotangent,
):
    place = Place(dp, seq)
    everyone = dp * seq
    _, count, width = tokens.shape
    hidden_own = up_weight.shape[1] // seq
    heads = HEADS // seq
    head_cols = heads * HEAD_DIM
    shard = qkv_weight.shape[0]
    ff_shard = down_weight.shape[0]
    length = segment_ids.shape[1]
    rows = tokens.reshape(count, width)

    qkv_cols = 3 * head_cols
    smalls = (query_bias, value_bias, out_bias, first_gain, first_shift, down_bias, second_gain, second_shift)
    up_rows = ff_shard // shard
    packed = jnp.concatenate([v.reshape(1, shard) for v in smalls] + [up_bias.reshape(up_rows, shard)])
    vector_count = packed.shape[0]
    qkv_blocks = qkv_weight.reshape(shard, 3, seq, head_cols).transpose(2, 0, 1, 3)
    up_blocks = up_weight.reshape(shard, dp, seq, ff_shard).transpose(2, 0, 1, 3)
    blocks = jnp.concatenate(
        [qkv_blocks.reshape(seq, shard, qkv_cols), up_blocks.reshape(seq, shard, hidden_own)], axis=2
    )
    extra = jnp.pad(packed, ((0, EXTRA - vector_count), (0, blocks.shape[2] - shard)))
    extra = jnp.broadcast_to(extra, (seq, *extra.shape))
    blocks = exchange_seq(place, jnp.concatenate([blocks, extra], axis=1))
    qkv_block = blocks[:, :shard, :qkv_cols].reshape(seq * shard, qkv_cols)
    up_block = blocks[:, :shard, qkv_cols:].reshape(seq * shard, hidden_own)
    packed_seq = blocks[:, shard:, :shard].transpose(1, 0, 2).reshape(EXTRA, seq * shard)
    packed_seq = jnp.pad(packed_seq, ((0, 0), (0, head_cols - seq * shard)))
    out_x = jnp.zeros((place.nx, shard, width), BF16)
    for k in range(place.nx):
        here = out_weight if k == 0 else place.to_x(out_weight, k)
        out_x = put(out_x, here, (place.x - k) % place.nx)
    out_x = out_x.reshape(place.nx * shard, width)

    def columns(a):
        return [a[:, i : i + head_cols] for i in range(0, a.shape[1], head_cols)]

    stack = [(0, b, i * head_cols) for i, b in enumerate(columns(qkv_block))]
    stack += [(1, b, i * head_cols) for i, b in enumerate(columns(out_x))]
    stack += [(2, packed_seq, 0)]
    pieces, at = [], 0
    for i, b, col in stack:
        pieces.append((i, at, b.shape[0], col))
        at += b.shape[0]
    attention = Gather(place, jnp.concatenate([b for _, b, _ in stack], axis=0))
    attention.start()
    for step in range(place.nz - 1):
        attention.settle()
        if step == place.nz - 3:
            early = attention.here
    up_block, down_late, _ = lax.optimization_barrier((up_block, down_weight, early))
    full_up = lax.all_gather(up_block, "dp", axis=0, tiled=True)
    full_down = lax.all_gather(down_late, "dp", axis=0, tiled=True)
    attention.settle()
    full_qkv, packed_all = attention.finish(
        [(i // 2, *rest) for i, *rest in pieces if i != 1], ((seq * shard, qkv_cols), (EXTRA, head_cols))
    )
    (out_half,) = attention.finish(
        [(0, *rest) for i, *rest in pieces if i == 1], ((place.nx * shard, width),)
    )
    out_half = out_half.reshape(dp * place.nx, 1, shard, width)
    full_out = place.pair(out_half, place.core(out_half), 1).reshape(width, width)
    full_qkv = full_qkv.reshape(width, qkv_cols)
    packed_all = packed_all[:, :vector_count, : seq * shard].astype(F32)
    vectors = [packed_all[:, i].reshape(1, width) for i in range(len(smalls))]
    full_query, full_value, bias_out, gain_one, shift_one, bias_down, gain_two, shift_two = vectors
    bias_up = packed_all[:, len(smalls) :].reshape(dp, up_rows, seq, shard)
    bias_up = lax.dynamic_index_in_dim(bias_up, place.s, 2, keepdims=False).reshape(1, hidden_own)

    row_blocks, _ = rows_each(place, rows, lambda k, block: ())
    all_rows = jnp.zeros((place.nx, CORES * count, width), BF16)
    for k, both in enumerate(row_blocks):
        mine, other = both[:count], both[count:]
        all_rows = put(all_rows, place.pair(mine, other, 0), (place.x + k) % place.nx)
    all_rows = all_rows.reshape(length, width)

    seg_row = segment_ids
    seg_col = segment_ids.reshape(length, 1)
    blocks = length // BLOCK
    ids = segment_ids.reshape(length)
    heads_first = ids[::BLOCK]
    heads_last = ids[BLOCK - 1 :: BLOCK]
    low = jnp.sum(ids[None, :] < heads_first[:, None], axis=1, dtype=jnp.int32)
    high = jnp.sum(ids[None, :] <= heads_last[:, None], axis=1, dtype=jnp.int32)
    bounds = jnp.concatenate([low // BLOCK, (high + BLOCK - 1) // BLOCK])
    own_cols = place.s * head_cols
    query_own = lax.dynamic_slice_in_dim(full_query, own_cols, head_cols, 1)
    value_own = lax.dynamic_slice_in_dim(full_value, own_cols, head_cols, 1)
    qkv_bias = jnp.concatenate([query_own, jnp.zeros_like(query_own), value_own], axis=1)
    qkv = (matmul(all_rows, full_qkv) + qkv_bias).astype(BF16)
    mixed_own, logs = attend(qkv, seg_row, seg_col, bounds, heads)

    mixed = exchange_seq(place, mixed_own.reshape(seq, count, head_cols))
    mixed = mixed.transpose(1, 0, 2).reshape(count, width)
    branch = matmul(mixed, full_out) + bias_out
    first, normed_one, factor_one = norm_forward(rows.astype(F32) + branch, gain_one, shift_one)
    first_low = first.astype(BF16)
    first_all, hidden_slopes = rows_each(
        place, first_low, lambda k, block: gelu_pair(matmul(block, full_up) + bias_up)
    )
    hidden_all = [hidden for hidden, _ in hidden_slopes]
    second = rows_sum(place, hidden_all, lambda hidden: matmul(hidden, full_down)) + bias_down
    result, normed_two, factor_two = norm_forward(first + second, gain_two, shift_two)
    output = result.astype(BF16).reshape(tokens.shape)

    grad_out = cotangent.reshape(count, width).astype(F32)
    second_grad, gain_two_grad, shift_two_grad = norm_backward(
        grad_out, normed_two, factor_two, gain_two
    )
    second_low = second_grad.astype(BF16)
    down_bias_grad = jnp.sum(second_low, axis=0, dtype=F32)
    second_all, preact_all = rows_each(
        place,
        second_low,
        lambda k, block: (
            right_product(block, full_down) * hidden_slopes[k][1].astype(F32)
        ).astype(BF16),
    )
    first_grad = second_grad + rows_sum(place, preact_all, lambda p: right_product(p, full_up))
    if hidden_own == width:
        both_grads = weight_grads(hidden_all, second_all, first_all, preact_all)
        both_owned = lax.psum_scatter(both_grads, "dp", scatter_dimension=0, tiled=True)
        down_owned, up_owned = both_owned[:, :width].astype(F32), both_owned[:, width:]
    else:
        down_grad = weight_grads(hidden_all, second_all)
        down_owned = lax.psum_scatter(down_grad, "dp", scatter_dimension=0, tiled=True).astype(F32)
        up_grad = weight_grads(first_all, preact_all)
        up_owned = lax.psum_scatter(up_grad, "dp", scatter_dimension=0, tiled=True)
    up_bias_grad = sum(jnp.sum(p, axis=0, dtype=F32) for p in preact_all)

    residual_grad, gain_one_grad, shift_one_grad = norm_backward(
        first_grad, normed_one, factor_one, gain_one
    )
    branch_low = residual_grad.astype(BF16)
    out_bias_grad = jnp.sum(branch_low, axis=0, dtype=F32)
    mixed_grad = right_product(branch_low, full_out).astype(BF16)
    grad_blocks = mixed_grad.reshape(count, seq, head_cols).transpose(1, 0, 2)
    grad_own = exchange_seq(place, grad_blocks).reshape(length, head_cols)

    up_bias_wide = lax.dynamic_update_index_in_dim(
        jnp.zeros((dp, seq, ff_shard), F32), up_bias_grad.reshape(dp, ff_shard), place.s, 1
    ).reshape(everyone, ff_shard)
    vector_sums = (
        out_bias_grad,
        gain_one_grad,
        shift_one_grad,
        down_bias_grad,
        gain_two_grad,
        shift_two_grad,
    )
    extra = jnp.concatenate([v.reshape(everyone, shard) for v in vector_sums] + [up_bias_wide], axis=1)
    wide_count = extra.shape[1]
    extra = jnp.pad(extra.astype(BF16)[:, None], ((0, 0), (0, EXTRA - 1), (0, width - wide_count)))
    out_grad = weight_grads([mixed], [branch_low]).reshape(everyone, shard, width)
    view = jnp.concatenate([out_grad, extra], axis=1)
    view = view.reshape(dp * place.nx, CORES, shard + EXTRA, width)
    mine = lax.dynamic_index_in_dim(view, place.c, 1, keepdims=False)
    other = lax.dynamic_index_in_dim(view, 1 - place.c, 1, keepdims=False)
    view = (mine.astype(F32) + place.core(other).astype(F32)).astype(BF16)
    view = view.reshape(dp, place.nx, shard + EXTRA, width)
    summed = lax.dynamic_index_in_dim(view, place.x, 1, keepdims=False).astype(F32)
    for k in range(1, place.nx):
        sent = lax.dynamic_index_in_dim(view, (place.x + k) % place.nx, 1, keepdims=False)
        summed = summed + place.to_x(sent, k).astype(F32)
    qkv_grad = attend_back(qkv, mixed_own, grad_own, logs, seg_row, seg_col, bounds, heads)
    qkv_grad, summed = lax.optimization_barrier((qkv_grad, summed))
    token_parts = right_product(qkv_grad, full_qkv).astype(BF16)
    token_parts = token_parts.reshape(place.nx, CORES, count, width)
    ordered = []
    for k in range(place.nx):
        both = take(token_parts, (place.x + k) % place.nx)
        ordered.append(
            jnp.concatenate([take(both, place.c), take(both, 1 - place.c)], axis=0)
        )
    token_sum = rows_sum(place, ordered, lambda v: v)
    joint_grad = weight_grads([all_rows], [qkv_grad])

    joint_grad = joint_grad.reshape(dp, seq * shard, qkv_cols)
    sums = jnp.sum(qkv_grad, axis=0, dtype=F32).reshape(3, head_cols)
    ends = jnp.stack([sums[0], sums[2]])
    ends = lax.dynamic_update_slice_in_dim(jnp.zeros((2, width), F32), ends, own_cols, 1)
    ends = ends.reshape(2, dp, seq * shard).transpose(1, 0, 2).reshape(dp, 1, 2 * seq * shard)
    ends = jnp.pad(ends.astype(BF16), ((0, 0), (0, EXTRA - 1), (0, head_cols - 2 * seq * shard)))
    views = [(joint_grad, i * head_cols, head_cols) for i in range(3)]
    views += [(ends, 0, head_cols)]
    views += [(summed.astype(BF16), i, head_cols) for i in range(0, width, head_cols)]
    owned = scatter_dp(place, views, token_sum)
    per = seq * shard
    joint = jnp.concatenate([owned[i * per : (i + 1) * per] for i in range(3)], axis=1).astype(BF16)
    ends = owned[3 * per]
    owned = owned[3 * per + EXTRA :].reshape(-1, shard + EXTRA, head_cols)
    out_owned = owned[:, :shard].transpose(1, 0, 2).reshape(shard, width)
    wide = owned[:, shard].reshape(width)
    out_bias_owned, gain_one_owned, shift_one_owned, down_bias_owned, gain_two_owned, shift_two_owned = [
        wide[i * shard : (i + 1) * shard] for i in range(len(vector_sums))
    ]
    up_bias_owned = wide[len(vector_sums) * shard : wide_count]
    ends = ends[: 2 * per].astype(BF16).reshape(2, seq, shard).transpose(1, 0, 2)
    ends = jnp.pad(
        ends.reshape(seq, 1, 2 * shard), ((0, 0), (0, EXTRA - 1), (0, qkv_cols - 2 * shard))
    )
    joint = jnp.concatenate([joint.reshape(seq, shard, qkv_cols), ends], axis=1)
    joint = exchange_seq(place, joint)
    up_owned, joint = lax.optimization_barrier((up_owned, joint))
    up_owned = up_owned.reshape(seq, shard, hidden_own)
    up_owned = exchange_seq(place, up_owned).reshape(seq, shard, dp, ff_shard)
    up_owned = up_owned.transpose(1, 2, 0, 3).reshape(up_weight.shape).astype(F32)
    joint_owned = joint[:, :shard].reshape(seq, shard, 3, head_cols).transpose(1, 2, 0, 3)
    joint_owned = joint_owned.reshape(qkv_weight.shape).astype(F32)
    ends = jnp.sum(joint[:, shard, : 2 * shard].astype(F32), axis=0).reshape(2, shard)

    tokens_grad = (residual_grad + token_sum).astype(BF16).reshape(tokens.shape)
    return (
        output,
        tokens_grad,
        joint_owned,
        ends[0],
        ends[1],
        out_owned,
        out_bias_owned,
        gain_one_owned,
        shift_one_owned,
        up_owned,
        up_bias_owned,
        down_owned,
        down_bias_owned,
        gain_two_owned,
        shift_two_owned,
    )


def solution(mesh):
    rows = P("dp", "seq", None)
    matrix = P(("dp", "seq"), None)
    vector = P(("dp", "seq"))
    params = (
        matrix,
        vector,
        vector,
        matrix,
        vector,
        vector,
        vector,
        matrix,
        vector,
        matrix,
        vector,
        vector,
        vector,
    )
    return jax.shard_map(
        partial(body, mesh.shape["dp"], mesh.shape["seq"]),
        mesh=mesh,
        in_specs=(rows, P("dp", None), *params, rows),
        out_specs=(rows, rows, *params),
        check_vma=False,
    )
```

```python
from functools import partial

import jax
import jax.numpy as jnp
from jax import lax
from jax.experimental import pallas as pl
from jax.experimental.pallas import tpu as pltpu
from jax.sharding import PartitionSpec as P

HEADS = 16
HEAD_DIM = 64
EPSILON = 1e-06
MASKED = -1e30
CORES = 2
EXTRA = 16
VMEM = pl.BlockSpec(memory_space=pltpu.VMEM)
F32 = jnp.float32
BF16 = jnp.bfloat16
DN_T = (((1,), (1,)), ((), ()))
DN_L = (((0,), (0,)), ((), ()))


def matmul(left, right):
    return jnp.dot(left, right, preferred_element_type=F32)


def left_product(left, right):
    return lax.dot_general(left, right, DN_L, preferred_element_type=F32)


def right_product(left, right):
    return lax.dot_general(left, right, DN_T, preferred_element_type=F32)


def norm_forward(value, gain, shift):
    mean = jnp.mean(value, axis=-1, keepdims=True)
    centered = value - mean
    variance = jnp.mean(centered * centered, axis=-1, keepdims=True)
    factor = lax.rsqrt(variance + EPSILON)
    normed = centered * factor
    return (normed * gain + shift, normed, factor)


def norm_backward(grad, normed, factor, gain):
    scaled = grad * gain
    inner = jnp.mean(scaled, axis=-1, keepdims=True)
    along = jnp.mean(scaled * normed, axis=-1, keepdims=True)
    return (
        factor * (scaled - inner - normed * along),
        jnp.sum(grad * normed, axis=0),
        jnp.sum(grad, axis=0),
    )


class Place:
    def __init__(self, dp, seq):
        self.dp, self.seq = dp, seq
        self.nx = seq // CORES
        self.ny = min(self.nx, dp)
        self.nz = dp // self.ny
        d = lax.axis_index("dp")
        s = lax.axis_index("seq")
        self.d, self.s = d, s
        self.z, self.y = d // self.ny, d % self.ny
        self.x, self.c = s // CORES, s % CORES

    def core(self, a):
        return lax.ppermute(a, "seq", [(i, i ^ 1) for i in range(self.seq)])

    def to_x(self, a, k):
        n = self.nx
        return lax.ppermute(
            a,
            "seq",
            [(i, ((i // CORES + k) % n) * CORES + i % CORES) for i in range(self.seq)],
        )

    def to_y(self, a, k):
        n = self.ny
        return lax.ppermute(
            a, "dp", [(i, i // n * n + (i % n + k) % n) for i in range(self.dp)]
        )

    def to_z(self, a, k):
        n, m = self.nz, self.ny
        return lax.ppermute(
            a, "dp", [(i, (i // m + k) % n * m + i % m) for i in range(self.dp)]
        )

    def pair(self, own, other, axis):
        first = jnp.where(self.c == 0, own, other)
        second = jnp.where(self.c == 0, other, own)
        return jnp.concatenate([first, second], axis=axis)


def put(buffer, block, index):
    return lax.dynamic_update_slice_in_dim(buffer, block[None], index, 0)


def take(buffer, index):
    return lax.dynamic_index_in_dim(buffer, index, 0, keepdims=False)


def exchange_seq(place, blocks):
    n = place.nx
    view = blocks.reshape(n, CORES, *blocks.shape[1:])
    arrived = []
    for k in range(n):
        send = take(view, (place.x + k) % n)
        arrived.append(place.to_x(send, k) if k else send)
    arrived = jnp.stack(arrived)
    mine = lax.dynamic_index_in_dim(arrived, place.c, 1, keepdims=True)
    other = place.core(lax.dynamic_index_in_dim(arrived, 1 - place.c, 1, keepdims=True))
    both = place.pair(mine, other, 1)
    ordered = jnp.stack([take(both, (place.x - source) % n) for source in range(n)])
    return ordered.reshape(blocks.shape)


def assemble_kernel(plan, counts, where, *refs):
    blocks, outs = refs[: len(plan)], refs[len(plan) :]
    ny, nz = counts
    for block, (k, j, pieces) in zip(blocks, plan):
        owner = lax.rem(where[0] - k + nz, nz) * ny + lax.rem(where[1] - j + ny, ny)
        for i, start, size, col in pieces:
            outs[i][pl.ds(owner, 1), :, col : col + block.shape[1]] = block[start : start + size][None]


class Gather:
    def __init__(self, place, block):
        self.place, self.here, self.k = place, block, 0
        self.blocks = [(0, 0, block)]

    def start(self):
        p = self.place
        self.sent = [p.to_y(self.here, j) for j in range(1, p.ny)]
        self.after = p.to_z(self.here, 1) if self.k < p.nz - 1 else self.here

    def settle(self):
        if self.k == self.place.nz:
            return
        sent, after = lax.optimization_barrier((self.sent, self.after))
        self.blocks += [(self.k, j + 1, b) for j, b in enumerate(sent)]
        self.k += 1
        self.here = after
        if self.k < self.place.nz:
            self.blocks.append((self.k, 0, after))
            self.start()

    def finish(self, pieces, shapes):
        p = self.place
        plan = [(k, j, pieces) for k, j, _ in self.blocks]
        return pl.pallas_call(
            partial(assemble_kernel, plan, (p.ny, p.nz)),
            in_specs=[pl.BlockSpec(memory_space=pltpu.SMEM)] + [VMEM] * len(plan),
            out_specs=[VMEM] * len(shapes),
            out_shape=[jax.ShapeDtypeStruct((p.ny * p.nz, *shape), BF16) for shape in shapes],
            compiler_params=pltpu.CompilerParams(vmem_limit_bytes=32 << 20),
        )(jnp.stack([p.z, p.y]), *[b for _, _, b in self.blocks])


def scatter_dp(place, views, beside):
    ny, nz = place.ny, place.nz

    def piece(z, y):
        return jnp.concatenate(
            [take(v, z * ny + y)[:, c : c + n] for v, c, n in views], axis=0
        )

    total = None
    for k in range(1, nz + 1):
        z = (place.z - k) % nz
        part = piece(z, place.y).astype(F32)
        for j in range(1, ny):
            send = piece(z, (place.y + j) % ny)
            sent = place.to_y(send, j)
            part = part + sent.astype(F32)
        if total is not None:
            send = total.astype(BF16)
            sent = place.to_z(send, 1)
            part = part + sent.astype(F32)
        if k == nz - 1:
            part, _ = lax.optimization_barrier((part, beside))
        total = part
    return total


def rows_each(place, rows, work):
    sent = [place.to_x(rows, place.nx - k) for k in range(1, place.nx)]
    blocks, done = [], []
    for k in range(place.nx):
        here = rows
        if k:
            here, _ = lax.optimization_barrier((sent[k - 1], done[-1]))
        blocks.append(jnp.concatenate([here, place.core(here)], axis=0))
        done.append(work(k, blocks[-1]))
    return blocks, done


def rows_sum(place, values, part, beside=()):
    total, both = None, None
    for k in reversed(range(place.nx)):
        value = values[k]
        if both is not None:
            value, _ = lax.optimization_barrier((value, both))
        low = part(value).astype(BF16)
        half = low.shape[0] // 2
        both = low[:half].astype(F32) + place.core(low[half:]).astype(F32)
        term = both
        if k:
            both = both.astype(BF16)
            term, _ = lax.optimization_barrier((place.to_x(both, k), beside))
            term = term.astype(F32)
        total = term if total is None else total + term
    return total


BLOCK = 384


def attend_kernel(heads, bounds, qkv_ref, seg_row, seg_col, mixed_ref, log_ref):
    length = qkv_ref.shape[0]
    width = heads * HEAD_DIM
    i = pl.program_id(0)
    start = pl.multiple_of(i * BLOCK, BLOCK)
    cols = pl.ds(start, BLOCK)
    seg_q = seg_row[:, cols]
    queries = [
        qkv_ref[cols, h * HEAD_DIM : (h + 1) * HEAD_DIM] * BF16(HEAD_DIM**-0.5)
        for h in range(heads)
    ]

    def step(j, carry):
        rows = pl.ds(pl.multiple_of(j * BLOCK, BLOCK), BLOCK)
        same = seg_col[rows, :] == seg_q
        out = []
        for h in range(heads):
            high, total, acc = carry[h]
            keys = qkv_ref[rows, width + h * HEAD_DIM : width + (h + 1) * HEAD_DIM]
            values = qkv_ref[rows, 2 * width + h * HEAD_DIM : 2 * width + (h + 1) * HEAD_DIM]
            scores = lax.dot_general(keys, queries[h], DN_T, preferred_element_type=F32)
            scores = jnp.where(same, scores, MASKED)
            new = jnp.maximum(high, jnp.max(scores, axis=0, keepdims=True))
            weights = jnp.exp(scores - new)
            fade = jnp.exp(high - new)
            total = total * fade + jnp.sum(weights, axis=0, keepdims=True)
            acc = acc * fade + lax.dot_general(
                values, weights.astype(BF16), DN_L, preferred_element_type=F32
            )
            out.append((new, total, acc))
        return tuple(out)

    first = tuple(
        (
            jnp.full((1, BLOCK), MASKED, F32),
            jnp.zeros((1, BLOCK), F32),
            jnp.zeros((HEAD_DIM, BLOCK), F32),
        )
        for _ in range(heads)
    )
    done = lax.fori_loop(bounds[i], bounds[i + length // BLOCK], step, first)
    mixed = jnp.concatenate([acc / total for _, total, acc in done], axis=0)
    mixed_ref[...] = mixed.T.astype(BF16)
    log_ref[...] = jnp.concatenate([high + jnp.log(total) for high, total, _ in done], axis=0)


def attend_back_kernel(
    heads, bounds, qkv_ref, mixed_ref, grad_ref, log_ref, seg_row, seg_col, out_ref, acc_ref
):
    length = qkv_ref.shape[0]
    width = heads * HEAD_DIM
    scale = HEAD_DIM**-0.5
    i = pl.program_id(0)

    @pl.when(i == 0)
    def _():
        acc_ref[...] = jnp.zeros_like(acc_ref)

    start = pl.multiple_of(i * BLOCK, BLOCK)
    cols = pl.ds(start, BLOCK)
    seg_q = seg_row[:, cols]
    grads_all = grad_ref[cols, :]
    along = (grads_all.astype(F32) * mixed_ref[cols, :].astype(F32)).T
    along = [
        jnp.sum(along[h * HEAD_DIM : (h + 1) * HEAD_DIM], axis=0, keepdims=True)
        for h in range(heads)
    ]
    logs = [log_ref[h : h + 1, cols] for h in range(heads)]
    queries = [
        qkv_ref[cols, h * HEAD_DIM : (h + 1) * HEAD_DIM] * BF16(scale) for h in range(heads)
    ]
    grads = [grads_all[:, h * HEAD_DIM : (h + 1) * HEAD_DIM] for h in range(heads)]

    def step(j, carry):
        rows = pl.ds(pl.multiple_of(j * BLOCK, BLOCK), BLOCK)
        same = seg_col[rows, :] == seg_q
        out, key_parts, value_parts = [], [], []
        for h in range(heads):
            keys = qkv_ref[rows, width + h * HEAD_DIM : width + (h + 1) * HEAD_DIM]
            values = qkv_ref[rows, 2 * width + h * HEAD_DIM : 2 * width + (h + 1) * HEAD_DIM]
            scores = lax.dot_general(keys, queries[h], DN_T, preferred_element_type=F32)
            shares = jnp.exp(jnp.where(same, scores, MASKED) - logs[h])
            shares_grad = lax.dot_general(values, grads[h], DN_T, preferred_element_type=F32)
            score_low = (shares * (shares_grad - along[h])).astype(BF16)
            value_parts.append(matmul(shares.astype(BF16), grads[h]))
            key_parts.append(matmul(score_low, queries[h]))
            out.append(
                carry[h] + lax.dot_general(keys, score_low, DN_L, preferred_element_type=F32)
            )
        acc_ref[rows, :width] += jnp.concatenate(key_parts, axis=1)
        acc_ref[rows, width:] += jnp.concatenate(value_parts, axis=1)
        return tuple(out)

    first = tuple(jnp.zeros((HEAD_DIM, BLOCK), F32) for _ in range(heads))
    done = lax.fori_loop(bounds[i], bounds[i + length // BLOCK], step, first)
    out_ref[cols, :width] = (jnp.concatenate(done, axis=0) * scale).T.astype(BF16)

    @pl.when(i == length // BLOCK - 1)
    def _():
        out_ref[:, width:] = acc_ref[...].astype(BF16)


def attend(qkv, seg_row, seg_col, bounds, heads):
    length = qkv.shape[0]
    width = heads * HEAD_DIM
    return pl.pallas_call(
        partial(attend_kernel, heads),
        grid_spec=pltpu.PrefetchScalarGridSpec(
            num_scalar_prefetch=1,
            grid=(length // BLOCK,),
            in_specs=[VMEM, VMEM, VMEM],
            out_specs=[
                pl.BlockSpec((BLOCK, width), lambda i, b: (i, 0)),
                pl.BlockSpec((heads, BLOCK), lambda i, b: (0, i)),
            ],
        ),
        out_shape=[
            jax.ShapeDtypeStruct((length, width), BF16),
            jax.ShapeDtypeStruct((heads, length), F32),
        ],
        compiler_params=pltpu.CompilerParams(vmem_limit_bytes=40 << 20),
        cost_estimate=pl.CostEstimate(
            flops=4 * length * length * width,
            bytes_accessed=8 * length * width,
            transcendentals=length * length * heads,
        ),
    )(bounds, qkv, seg_row, seg_col)


def attend_back(qkv, mixed, grad, logs, seg_row, seg_col, bounds, heads):
    length = qkv.shape[0]
    width = heads * HEAD_DIM
    return pl.pallas_call(
        partial(attend_back_kernel, heads),
        grid_spec=pltpu.PrefetchScalarGridSpec(
            num_scalar_prefetch=1,
            grid=(length // BLOCK,),
            in_specs=[VMEM] * 6,
            out_specs=VMEM,
            scratch_shapes=[pltpu.VMEM((length, 2 * width), F32)],
        ),
        out_shape=jax.ShapeDtypeStruct((length, 3 * width), BF16),
        compiler_params=pltpu.CompilerParams(vmem_limit_bytes=40 << 20),
        cost_estimate=pl.CostEstimate(
            flops=10 * length * length * width,
            bytes_accessed=16 * length * width,
            transcendentals=length * length * heads,
        ),
    )(bounds, qkv, mixed, grad, logs, seg_row, seg_col)


TILE = 256


def grads_kernel(count, *refs):
    out_ref = refs[-1]
    at = 0
    for i in range(0, len(refs) - 1, 2 * count):
        lefts, rights = refs[i : i + count], refs[i + count : i + 2 * count]
        cols = rights[0].shape[1]
        total = sum(left_product(a[...], b[...]) for a, b in zip(lefts, rights))
        out_ref[:, at : at + cols] = total.astype(BF16)
        at += cols


def weight_grads(*sides):
    count = len(sides[0])
    inner = sides[0][0].shape[1]
    cols = sum(rights[0].shape[1] for rights in sides[1::2])
    tile = min(TILE, inner)
    specs, values = [], []
    for n, side in enumerate(sides):
        for v in side:
            values.append(v)
            if n % 2:
                specs.append(VMEM)
            else:
                specs.append(pl.BlockSpec((v.shape[0], tile), lambda i: (0, i)))
    rows = sum(v.shape[0] for v in sides[0])
    return pl.pallas_call(
        partial(grads_kernel, count),
        grid=(inner // tile,),
        in_specs=specs,
        out_specs=pl.BlockSpec((tile, cols), lambda i: (i, 0)),
        out_shape=jax.ShapeDtypeStruct((inner, cols), BF16),
        compiler_params=pltpu.CompilerParams(vmem_limit_bytes=40 << 20),
        cost_estimate=pl.CostEstimate(
            flops=2 * rows * inner * cols,
            bytes_accessed=2 * sum(v.size for v in values) + 2 * inner * cols,
            transcendentals=0,
        ),
    )(*values)


def gelu_pair(preact):
    half = 0.5 + 0.5 * lax.erf(preact * (2.0**-0.5))
    slope = half + preact * jnp.exp(-0.5 * preact * preact) * 0.3989422804014327
    return (preact * half).astype(BF16), slope.astype(BF16)


def body(
    dp,
    seq,
    tokens,
    segment_ids,
    qkv_weight,
    query_bias,
    value_bias,
    out_weight,
    out_bias,
    first_gain,
    first_shift,
    up_weight,
    up_bias,
    down_weight,
    down_bias,
    second_gain,
    second_shift,
    cotangent,
):
    place = Place(dp, seq)
    everyone = dp * seq
    _, count, width = tokens.shape
    hidden_own = up_weight.shape[1] // seq
    heads = HEADS // seq
    head_cols = heads * HEAD_DIM
    shard = qkv_weight.shape[0]
    ff_shard = down_weight.shape[0]
    length = segment_ids.shape[1]
    rows = tokens.reshape(count, width)

    qkv_cols = 3 * head_cols
    smalls = (query_bias, value_bias, out_bias, first_gain, first_shift, down_bias, second_gain, second_shift)
    up_rows = ff_shard // shard
    packed = jnp.concatenate([v.reshape(1, shard) for v in smalls] + [up_bias.reshape(up_rows, shard)])
    vector_count = packed.shape[0]
    qkv_blocks = qkv_weight.reshape(shard, 3, seq, head_cols).transpose(2, 0, 1, 3)
    up_blocks = up_weight.reshape(shard, dp, seq, ff_shard).transpose(2, 0, 1, 3)
    blocks = jnp.concatenate(
        [qkv_blocks.reshape(seq, shard, qkv_cols), up_blocks.reshape(seq, shard, hidden_own)], axis=2
    )
    extra = jnp.pad(packed, ((0, EXTRA - vector_count), (0, blocks.shape[2] - shard)))
    extra = jnp.broadcast_to(extra, (seq, *extra.shape))
    blocks = exchange_seq(place, jnp.concatenate([blocks, extra], axis=1))
    qkv_block = blocks[:, :shard, :qkv_cols].reshape(seq * shard, qkv_cols)
    up_block = blocks[:, :shard, qkv_cols:].reshape(seq * shard, hidden_own)
    packed_seq = blocks[:, shard:, :shard].transpose(1, 0, 2).reshape(EXTRA, seq * shard)
    packed_seq = jnp.pad(packed_seq, ((0, 0), (0, head_cols - seq * shard)))
    out_x = jnp.zeros((place.nx, shard, width), BF16)
    for k in range(place.nx):
        here = out_weight if k == 0 else place.to_x(out_weight, k)
        out_x = put(out_x, here, (place.x - k) % place.nx)
    out_x = out_x.reshape(place.nx * shard, width)

    def columns(a):
        return [a[:, i : i + head_cols] for i in range(0, a.shape[1], head_cols)]

    stack = [(0, b, i * head_cols) for i, b in enumerate(columns(qkv_block))]
    stack += [(1, b, i * head_cols) for i, b in enumerate(columns(out_x))]
    stack += [(2, packed_seq, 0)]
    pieces, at = [], 0
    for i, b, col in stack:
        pieces.append((i, at, b.shape[0], col))
        at += b.shape[0]
    attention = Gather(place, jnp.concatenate([b for _, b, _ in stack], axis=0))
    attention.start()
    for step in range(place.nz - 1):
        attention.settle()
        if step == place.nz - 4:
            early = attention.here
    up_block, down_block, _ = lax.optimization_barrier((up_block, down_weight, early))
    if hidden_own == width:
        later = lax.all_gather(jnp.concatenate([up_block, down_block], axis=0), "dp", axis=0)
        full_up = later[:, : seq * shard].reshape(width, hidden_own)
        full_down = later[:, seq * shard :].reshape(hidden_own, width)
    else:
        full_up = lax.all_gather(up_block, "dp", axis=0, tiled=True)
        full_down = lax.all_gather(down_block, "dp", axis=0, tiled=True)
    attention.settle()
    full_qkv, packed_all = attention.finish(
        [(i // 2, *rest) for i, *rest in pieces if i != 1], ((seq * shard, qkv_cols), (EXTRA, head_cols))
    )
    (out_half,) = attention.finish(
        [(0, *rest) for i, *rest in pieces if i == 1], ((place.nx * shard, width),)
    )
    out_half = out_half.reshape(dp * place.nx, 1, shard, width)
    full_out = place.pair(out_half, place.core(out_half), 1).reshape(width, width)
    full_qkv = full_qkv.reshape(width, qkv_cols)
    packed_all = packed_all[:, :vector_count, : seq * shard].astype(F32)
    vectors = [packed_all[:, i].reshape(1, width) for i in range(len(smalls))]
    full_query, full_value, bias_out, gain_one, shift_one, bias_down, gain_two, shift_two = vectors
    bias_up = packed_all[:, len(smalls) :].reshape(dp, up_rows, seq, shard)
    bias_up = lax.dynamic_index_in_dim(bias_up, place.s, 2, keepdims=False).reshape(1, hidden_own)

    row_blocks, _ = rows_each(place, rows, lambda k, block: ())
    all_rows = jnp.zeros((place.nx, CORES * count, width), BF16)
    for k, both in enumerate(row_blocks):
        mine, other = both[:count], both[count:]
        all_rows = put(all_rows, place.pair(mine, other, 0), (place.x + k) % place.nx)
    all_rows = all_rows.reshape(length, width)

    seg_row = segment_ids
    seg_col = segment_ids.reshape(length, 1)
    blocks = length // BLOCK
    ids = segment_ids.reshape(length)
    heads_first = ids[::BLOCK]
    heads_last = ids[BLOCK - 1 :: BLOCK]
    low = jnp.sum(ids[None, :] < heads_first[:, None], axis=1, dtype=jnp.int32)
    high = jnp.sum(ids[None, :] <= heads_last[:, None], axis=1, dtype=jnp.int32)
    bounds = jnp.concatenate([low // BLOCK, (high + BLOCK - 1) // BLOCK])
    own_cols = place.s * head_cols
    query_own = lax.dynamic_slice_in_dim(full_query, own_cols, head_cols, 1)
    value_own = lax.dynamic_slice_in_dim(full_value, own_cols, head_cols, 1)
    qkv_bias = jnp.concatenate([query_own, jnp.zeros_like(query_own), value_own], axis=1)
    qkv = (matmul(all_rows, full_qkv) + qkv_bias).astype(BF16)
    mixed_own, logs = attend(qkv, seg_row, seg_col, bounds, heads)

    mixed = exchange_seq(place, mixed_own.reshape(seq, count, head_cols))
    mixed = mixed.transpose(1, 0, 2).reshape(count, width)
    branch = matmul(mixed, full_out) + bias_out
    first, normed_one, factor_one = norm_forward(rows.astype(F32) + branch, gain_one, shift_one)
    first_low = first.astype(BF16)
    first_all, hidden_slopes = rows_each(
        place, first_low, lambda k, block: gelu_pair(matmul(block, full_up) + bias_up)
    )
    hidden_all = [hidden for hidden, _ in hidden_slopes]
    second = rows_sum(place, hidden_all, lambda hidden: matmul(hidden, full_down)) + bias_down
    result, normed_two, factor_two = norm_forward(first + second, gain_two, shift_two)
    output = result.astype(BF16).reshape(tokens.shape)

    grad_out = cotangent.reshape(count, width).astype(F32)
    second_grad, gain_two_grad, shift_two_grad = norm_backward(
        grad_out, normed_two, factor_two, gain_two
    )
    second_low = second_grad.astype(BF16)
    down_bias_grad = jnp.sum(second_low, axis=0, dtype=F32)
    second_all, preact_all = rows_each(
        place,
        second_low,
        lambda k, block: (
            right_product(block, full_down) * hidden_slopes[k][1].astype(F32)
        ).astype(BF16),
    )
    if hidden_own == width:
        beside = weight_grads(hidden_all, second_all, first_all, preact_all)
        both_owned = lax.psum_scatter(beside, "dp", scatter_dimension=0, tiled=True)
        down_owned, up_owned = both_owned[:, :width].astype(F32), both_owned[:, width:]
    else:
        down_grad = weight_grads(hidden_all, second_all)
        down_owned = lax.psum_scatter(down_grad, "dp", scatter_dimension=0, tiled=True).astype(F32)
        beside = weight_grads(first_all, preact_all)
        up_owned = lax.psum_scatter(beside, "dp", scatter_dimension=0, tiled=True)
    first_grad = second_grad + rows_sum(
        place, preact_all, lambda p: right_product(p, full_up), beside
    )
    up_bias_grad = sum(jnp.sum(p, axis=0, dtype=F32) for p in preact_all)

    residual_grad, gain_one_grad, shift_one_grad = norm_backward(
        first_grad, normed_one, factor_one, gain_one
    )
    branch_low = residual_grad.astype(BF16)
    out_bias_grad = jnp.sum(branch_low, axis=0, dtype=F32)
    mixed_grad = right_product(branch_low, full_out).astype(BF16)
    grad_blocks = mixed_grad.reshape(count, seq, head_cols).transpose(1, 0, 2)
    grad_own = exchange_seq(place, grad_blocks).reshape(length, head_cols)

    up_bias_wide = lax.dynamic_update_index_in_dim(
        jnp.zeros((dp, seq, ff_shard), F32), up_bias_grad.reshape(dp, ff_shard), place.s, 1
    ).reshape(everyone, ff_shard)
    vector_sums = (
        out_bias_grad,
        gain_one_grad,
        shift_one_grad,
        down_bias_grad,
        gain_two_grad,
        shift_two_grad,
    )
    extra = jnp.concatenate([v.reshape(everyone, shard) for v in vector_sums] + [up_bias_wide], axis=1)
    wide_count = extra.shape[1]
    extra = jnp.pad(extra.astype(BF16)[:, None], ((0, 0), (0, EXTRA - 1), (0, width - wide_count)))
    branch_late, _ = lax.optimization_barrier((branch_low, mixed_grad))
    out_grad = weight_grads([mixed], [branch_late]).reshape(everyone, shard, width)
    view = jnp.concatenate([out_grad, extra], axis=1)
    view = view.reshape(dp * place.nx, CORES, shard + EXTRA, width)
    mine = lax.dynamic_index_in_dim(view, place.c, 1, keepdims=False)
    other = lax.dynamic_index_in_dim(view, 1 - place.c, 1, keepdims=False)
    view = (mine.astype(F32) + place.core(other).astype(F32)).astype(BF16)
    view = view.reshape(dp, place.nx, shard + EXTRA, width)
    summed = lax.dynamic_index_in_dim(view, place.x, 1, keepdims=False).astype(F32)
    for k in range(1, place.nx):
        sent = lax.dynamic_index_in_dim(view, (place.x + k) % place.nx, 1, keepdims=False)
        summed = summed + place.to_x(sent, k).astype(F32)
    qkv_grad = attend_back(qkv, mixed_own, grad_own, logs, seg_row, seg_col, bounds, heads)
    qkv_grad, summed = lax.optimization_barrier((qkv_grad, summed))
    token_parts = right_product(qkv_grad, full_qkv).astype(BF16)
    token_parts = token_parts.reshape(place.nx, CORES, count, width)
    ordered = []
    for k in range(place.nx):
        both = take(token_parts, (place.x + k) % place.nx)
        ordered.append(
            jnp.concatenate([take(both, place.c), take(both, 1 - place.c)], axis=0)
        )
    token_sum = rows_sum(place, ordered, lambda v: v)
    joint_grad = weight_grads([all_rows], [qkv_grad])

    joint_grad = joint_grad.reshape(dp, seq * shard, qkv_cols)
    sums = jnp.sum(qkv_grad, axis=0, dtype=F32).reshape(3, head_cols)
    ends = jnp.stack([sums[0], sums[2]])
    ends = lax.dynamic_update_slice_in_dim(jnp.zeros((2, width), F32), ends, own_cols, 1)
    ends = ends.reshape(2, dp, seq * shard).transpose(1, 0, 2).reshape(dp, 1, 2 * seq * shard)
    ends = jnp.pad(ends.astype(BF16), ((0, 0), (0, EXTRA - 1), (0, head_cols - 2 * seq * shard)))
    views = [(joint_grad, i * head_cols, head_cols) for i in range(3)]
    views += [(ends, 0, head_cols)]
    views += [(summed.astype(BF16), i, head_cols) for i in range(0, width, head_cols)]
    owned = scatter_dp(place, views, token_sum)
    per = seq * shard
    joint = jnp.concatenate([owned[i * per : (i + 1) * per] for i in range(3)], axis=1).astype(BF16)
    ends = owned[3 * per]
    owned = owned[3 * per + EXTRA :].reshape(-1, shard + EXTRA, head_cols)
    out_owned = owned[:, :shard].transpose(1, 0, 2).reshape(shard, width)
    wide = owned[:, shard].reshape(width)
    out_bias_owned, gain_one_owned, shift_one_owned, down_bias_owned, gain_two_owned, shift_two_owned = [
        wide[i * shard : (i + 1) * shard] for i in range(len(vector_sums))
    ]
    up_bias_owned = wide[len(vector_sums) * shard : wide_count]
    ends = ends[: 2 * per].astype(BF16).reshape(2, seq, shard).transpose(1, 0, 2)
    ends = jnp.pad(
        ends.reshape(seq, 1, 2 * shard), ((0, 0), (0, EXTRA - 1), (0, qkv_cols - 2 * shard))
    )
    joint = jnp.concatenate([joint.reshape(seq, shard, qkv_cols), ends], axis=1)
    joint = exchange_seq(place, joint)
    up_owned, joint = lax.optimization_barrier((up_owned, joint))
    up_owned = up_owned.reshape(seq, shard, hidden_own)
    up_owned = exchange_seq(place, up_owned).reshape(seq, shard, dp, ff_shard)
    up_owned = up_owned.transpose(1, 2, 0, 3).reshape(up_weight.shape).astype(F32)
    joint_owned = joint[:, :shard].reshape(seq, shard, 3, head_cols).transpose(1, 2, 0, 3)
    joint_owned = joint_owned.reshape(qkv_weight.shape).astype(F32)
    ends = jnp.sum(joint[:, shard, : 2 * shard].astype(F32), axis=0).reshape(2, shard)

    tokens_grad = (residual_grad + token_sum).astype(BF16).reshape(tokens.shape)
    return (
        output,
        tokens_grad,
        joint_owned,
        ends[0],
        ends[1],
        out_owned,
        out_bias_owned,
        gain_one_owned,
        shift_one_owned,
        up_owned,
        up_bias_owned,
        down_owned,
        down_bias_owned,
        gain_two_owned,
        shift_two_owned,
    )


def solution(mesh):
    rows = P("dp", "seq", None)
    matrix = P(("dp", "seq"), None)
    vector = P(("dp", "seq"))
    params = (
        matrix,
        vector,
        vector,
        matrix,
        vector,
        vector,
        vector,
        matrix,
        vector,
        matrix,
        vector,
        vector,
        vector,
    )
    return jax.shard_map(
        partial(body, mesh.shape["dp"], mesh.shape["seq"]),
        mesh=mesh,
        in_specs=(rows, P("dp", None), *params, rows),
        out_specs=(rows, rows, *params),
        check_vma=False,
    )
```

```python
from functools import partial

import jax
import jax.numpy as jnp
from jax import lax
from jax.experimental import pallas as pl
from jax.experimental.pallas import tpu as pltpu
from jax.sharding import PartitionSpec as P

HEADS = 16
HEAD_DIM = 64
EPSILON = 1e-06
MASKED = -1e30
CORES = 2
EXTRA = 16
VMEM = pl.BlockSpec(memory_space=pltpu.VMEM)
F32 = jnp.float32
BF16 = jnp.bfloat16
DN_T = (((1,), (1,)), ((), ()))
DN_L = (((0,), (0,)), ((), ()))


def matmul(left, right):
    return jnp.dot(left, right, preferred_element_type=F32)


def left_product(left, right):
    return lax.dot_general(left, right, DN_L, preferred_element_type=F32)


def right_product(left, right):
    return lax.dot_general(left, right, DN_T, preferred_element_type=F32)


def norm_forward(value, gain, shift):
    mean = jnp.mean(value, axis=-1, keepdims=True)
    centered = value - mean
    variance = jnp.mean(centered * centered, axis=-1, keepdims=True)
    factor = lax.rsqrt(variance + EPSILON)
    normed = centered * factor
    return (normed * gain + shift, normed, factor)


def norm_backward(grad, normed, factor, gain):
    scaled = grad * gain
    inner = jnp.mean(scaled, axis=-1, keepdims=True)
    along = jnp.mean(scaled * normed, axis=-1, keepdims=True)
    return (
        factor * (scaled - inner - normed * along),
        jnp.sum(grad * normed, axis=0),
        jnp.sum(grad, axis=0),
    )


class Place:
    def __init__(self, dp, seq):
        self.dp, self.seq = dp, seq
        self.nx = seq // CORES
        self.ny = min(self.nx, dp)
        self.nz = dp // self.ny
        d = lax.axis_index("dp")
        s = lax.axis_index("seq")
        self.d, self.s = d, s
        self.z, self.y = d // self.ny, d % self.ny
        self.x, self.c = s // CORES, s % CORES

    def core(self, a):
        return lax.ppermute(a, "seq", [(i, i ^ 1) for i in range(self.seq)])

    def to_x(self, a, k):
        n = self.nx
        return lax.ppermute(
            a,
            "seq",
            [(i, ((i // CORES + k) % n) * CORES + i % CORES) for i in range(self.seq)],
        )

    def to_y(self, a, k):
        n = self.ny
        return lax.ppermute(
            a, "dp", [(i, i // n * n + (i % n + k) % n) for i in range(self.dp)]
        )

    def to_z(self, a, k):
        n, m = self.nz, self.ny
        return lax.ppermute(
            a, "dp", [(i, (i // m + k) % n * m + i % m) for i in range(self.dp)]
        )

    def pair(self, own, other, axis):
        first = jnp.where(self.c == 0, own, other)
        second = jnp.where(self.c == 0, other, own)
        return jnp.concatenate([first, second], axis=axis)


def put(buffer, block, index):
    return lax.dynamic_update_slice_in_dim(buffer, block[None], index, 0)


def take(buffer, index):
    return lax.dynamic_index_in_dim(buffer, index, 0, keepdims=False)


def exchange_seq(place, blocks):
    n = place.nx
    view = blocks.reshape(n, CORES, *blocks.shape[1:])
    arrived = []
    for k in range(n):
        send = take(view, (place.x + k) % n)
        arrived.append(place.to_x(send, k) if k else send)
    arrived = jnp.stack(arrived)
    mine = lax.dynamic_index_in_dim(arrived, place.c, 1, keepdims=True)
    other = place.core(lax.dynamic_index_in_dim(arrived, 1 - place.c, 1, keepdims=True))
    both = place.pair(mine, other, 1)
    ordered = jnp.stack([take(both, (place.x - source) % n) for source in range(n)])
    return ordered.reshape(blocks.shape)


def assemble_kernel(plan, counts, where, *refs):
    blocks, outs = refs[: len(plan)], refs[len(plan) :]
    ny, nz = counts
    for block, (k, j, pieces) in zip(blocks, plan):
        owner = lax.rem(where[0] - k + nz, nz) * ny + lax.rem(where[1] - j + ny, ny)
        for i, start, size, col in pieces:
            outs[i][pl.ds(owner, 1), :, col : col + block.shape[1]] = block[start : start + size][None]


class Gather:
    def __init__(self, place, block):
        self.place, self.here, self.k = place, block, 0
        self.blocks = [(0, 0, block)]

    def start(self):
        p = self.place
        self.sent = [p.to_y(self.here, j) for j in range(1, p.ny)]
        self.after = p.to_z(self.here, 1) if self.k < p.nz - 1 else self.here

    def settle(self):
        if self.k == self.place.nz:
            return
        sent, after = lax.optimization_barrier((self.sent, self.after))
        self.blocks += [(self.k, j + 1, b) for j, b in enumerate(sent)]
        self.k += 1
        self.here = after
        if self.k < self.place.nz:
            self.blocks.append((self.k, 0, after))
            self.start()

    def finish(self, pieces, shapes):
        p = self.place
        plan = [(k, j, pieces) for k, j, _ in self.blocks]
        return pl.pallas_call(
            partial(assemble_kernel, plan, (p.ny, p.nz)),
            in_specs=[pl.BlockSpec(memory_space=pltpu.SMEM)] + [VMEM] * len(plan),
            out_specs=[VMEM] * len(shapes),
            out_shape=[jax.ShapeDtypeStruct((p.ny * p.nz, *shape), BF16) for shape in shapes],
            compiler_params=pltpu.CompilerParams(vmem_limit_bytes=32 << 20),
        )(jnp.stack([p.z, p.y]), *[b for _, _, b in self.blocks])


def scatter_dp(place, views, beside):
    ny, nz = place.ny, place.nz

    def piece(z, y):
        return jnp.concatenate(
            [take(v, z * ny + y)[:, c : c + n] for v, c, n in views], axis=0
        )

    total = None
    for k in range(1, nz + 1):
        z = (place.z - k) % nz
        part = piece(z, place.y).astype(F32)
        for j in range(1, ny):
            send = piece(z, (place.y + j) % ny)
            sent = place.to_y(send, j)
            part = part + sent.astype(F32)
        if total is not None:
            send = total.astype(BF16)
            sent = place.to_z(send, 1)
            part = part + sent.astype(F32)
        if k == nz - 1:
            part, _ = lax.optimization_barrier((part, beside))
        total = part
    return total


def rows_each(place, rows, work):
    sent = [place.to_x(rows, place.nx - k) for k in range(1, place.nx)]
    blocks, done = [], []
    for k in range(place.nx):
        here = rows
        if k:
            here, _ = lax.optimization_barrier((sent[k - 1], done[-1]))
        blocks.append(jnp.concatenate([here, place.core(here)], axis=0))
        done.append(work(k, blocks[-1]))
    return blocks, done


def rows_sum(place, values, part, beside=()):
    total, both = None, None
    for k in reversed(range(place.nx)):
        value = values[k]
        if both is not None:
            value, _ = lax.optimization_barrier((value, both))
        low = part(value).astype(BF16)
        half = low.shape[0] // 2
        both = low[:half].astype(F32) + place.core(low[half:]).astype(F32)
        term = both
        if k:
            both = both.astype(BF16)
            term, _ = lax.optimization_barrier((place.to_x(both, k), beside))
            term = term.astype(F32)
        total = term if total is None else total + term
    return total


BLOCK = 384


def attend_kernel(heads, bounds, qkv_ref, seg_row, seg_col, mixed_ref, log_ref):
    length = qkv_ref.shape[0]
    width = heads * HEAD_DIM
    i = pl.program_id(0)
    start = pl.multiple_of(i * BLOCK, BLOCK)
    cols = pl.ds(start, BLOCK)
    seg_q = seg_row[:, cols]
    queries = [
        qkv_ref[cols, h * HEAD_DIM : (h + 1) * HEAD_DIM] * BF16(HEAD_DIM**-0.5)
        for h in range(heads)
    ]

    def step(j, carry):
        rows = pl.ds(pl.multiple_of(j * BLOCK, BLOCK), BLOCK)
        same = seg_col[rows, :] == seg_q
        out = []
        for h in range(heads):
            high, total, acc = carry[h]
            keys = qkv_ref[rows, width + h * HEAD_DIM : width + (h + 1) * HEAD_DIM]
            values = qkv_ref[rows, 2 * width + h * HEAD_DIM : 2 * width + (h + 1) * HEAD_DIM]
            scores = lax.dot_general(keys, queries[h], DN_T, preferred_element_type=F32)
            scores = jnp.where(same, scores, MASKED)
            new = jnp.maximum(high, jnp.max(scores, axis=0, keepdims=True))
            weights = jnp.exp(scores - new)
            fade = jnp.exp(high - new)
            total = total * fade + jnp.sum(weights, axis=0, keepdims=True)
            acc = acc * fade + lax.dot_general(
                values, weights.astype(BF16), DN_L, preferred_element_type=F32
            )
            out.append((new, total, acc))
        return tuple(out)

    first = tuple(
        (
            jnp.full((1, BLOCK), MASKED, F32),
            jnp.zeros((1, BLOCK), F32),
            jnp.zeros((HEAD_DIM, BLOCK), F32),
        )
        for _ in range(heads)
    )
    done = lax.fori_loop(bounds[i], bounds[i + length // BLOCK], step, first)
    mixed = jnp.concatenate([acc / total for _, total, acc in done], axis=0)
    mixed_ref[...] = mixed.T.astype(BF16)
    log_ref[...] = jnp.concatenate([high + jnp.log(total) for high, total, _ in done], axis=0)


def attend_back_kernel(
    heads, bounds, qkv_ref, mixed_ref, grad_ref, log_ref, seg_row, seg_col, out_ref, acc_ref
):
    length = qkv_ref.shape[0]
    width = heads * HEAD_DIM
    scale = HEAD_DIM**-0.5
    i = pl.program_id(0)

    @pl.when(i == 0)
    def _():
        acc_ref[...] = jnp.zeros_like(acc_ref)

    start = pl.multiple_of(i * BLOCK, BLOCK)
    cols = pl.ds(start, BLOCK)
    seg_q = seg_row[:, cols]
    grads_all = grad_ref[cols, :]
    along = (grads_all.astype(F32) * mixed_ref[cols, :].astype(F32)).T
    along = [
        jnp.sum(along[h * HEAD_DIM : (h + 1) * HEAD_DIM], axis=0, keepdims=True)
        for h in range(heads)
    ]
    logs = [log_ref[h : h + 1, cols] for h in range(heads)]
    queries = [
        qkv_ref[cols, h * HEAD_DIM : (h + 1) * HEAD_DIM] * BF16(scale) for h in range(heads)
    ]
    grads = [grads_all[:, h * HEAD_DIM : (h + 1) * HEAD_DIM] for h in range(heads)]

    def step(j, carry):
        rows = pl.ds(pl.multiple_of(j * BLOCK, BLOCK), BLOCK)
        same = seg_col[rows, :] == seg_q
        out, key_parts, value_parts = [], [], []
        for h in range(heads):
            keys = qkv_ref[rows, width + h * HEAD_DIM : width + (h + 1) * HEAD_DIM]
            values = qkv_ref[rows, 2 * width + h * HEAD_DIM : 2 * width + (h + 1) * HEAD_DIM]
            scores = lax.dot_general(keys, queries[h], DN_T, preferred_element_type=F32)
            shares = jnp.exp(jnp.where(same, scores, MASKED) - logs[h])
            shares_grad = lax.dot_general(values, grads[h], DN_T, preferred_element_type=F32)
            score_low = (shares * (shares_grad - along[h])).astype(BF16)
            value_parts.append(matmul(shares.astype(BF16), grads[h]))
            key_parts.append(matmul(score_low, queries[h]))
            out.append(
                carry[h] + lax.dot_general(keys, score_low, DN_L, preferred_element_type=F32)
            )
        acc_ref[rows, :width] += jnp.concatenate(key_parts, axis=1)
        acc_ref[rows, width:] += jnp.concatenate(value_parts, axis=1)
        return tuple(out)

    first = tuple(jnp.zeros((HEAD_DIM, BLOCK), F32) for _ in range(heads))
    done = lax.fori_loop(bounds[i], bounds[i + length // BLOCK], step, first)
    out_ref[cols, :width] = (jnp.concatenate(done, axis=0) * scale).T.astype(BF16)

    @pl.when(i == length // BLOCK - 1)
    def _():
        out_ref[:, width:] = acc_ref[...].astype(BF16)


def attend(qkv, seg_row, seg_col, bounds, heads):
    length = qkv.shape[0]
    width = heads * HEAD_DIM
    return pl.pallas_call(
        partial(attend_kernel, heads),
        grid_spec=pltpu.PrefetchScalarGridSpec(
            num_scalar_prefetch=1,
            grid=(length // BLOCK,),
            in_specs=[VMEM, VMEM, VMEM],
            out_specs=[
                pl.BlockSpec((BLOCK, width), lambda i, b: (i, 0)),
                pl.BlockSpec((heads, BLOCK), lambda i, b: (0, i)),
            ],
        ),
        out_shape=[
            jax.ShapeDtypeStruct((length, width), BF16),
            jax.ShapeDtypeStruct((heads, length), F32),
        ],
        compiler_params=pltpu.CompilerParams(vmem_limit_bytes=40 << 20),
        cost_estimate=pl.CostEstimate(
            flops=4 * length * length * width,
            bytes_accessed=8 * length * width,
            transcendentals=length * length * heads,
        ),
    )(bounds, qkv, seg_row, seg_col)


def attend_back(qkv, mixed, grad, logs, seg_row, seg_col, bounds, heads):
    length = qkv.shape[0]
    width = heads * HEAD_DIM
    return pl.pallas_call(
        partial(attend_back_kernel, heads),
        grid_spec=pltpu.PrefetchScalarGridSpec(
            num_scalar_prefetch=1,
            grid=(length // BLOCK,),
            in_specs=[VMEM] * 6,
            out_specs=VMEM,
            scratch_shapes=[pltpu.VMEM((length, 2 * width), F32)],
        ),
        out_shape=jax.ShapeDtypeStruct((length, 3 * width), BF16),
        compiler_params=pltpu.CompilerParams(vmem_limit_bytes=40 << 20),
        cost_estimate=pl.CostEstimate(
            flops=10 * length * length * width,
            bytes_accessed=16 * length * width,
            transcendentals=length * length * heads,
        ),
    )(bounds, qkv, mixed, grad, logs, seg_row, seg_col)


TILE = 256


def grads_kernel(count, *refs):
    out_ref = refs[-1]
    at = 0
    for i in range(0, len(refs) - 1, 2 * count):
        lefts, rights = refs[i : i + count], refs[i + count : i + 2 * count]
        cols = rights[0].shape[1]
        total = sum(left_product(a[...], b[...]) for a, b in zip(lefts, rights))
        out_ref[:, at : at + cols] = total.astype(BF16)
        at += cols


def weight_grads(*sides):
    count = len(sides[0])
    inner = sides[0][0].shape[1]
    cols = sum(rights[0].shape[1] for rights in sides[1::2])
    tile = min(TILE, inner)
    specs, values = [], []
    for n, side in enumerate(sides):
        for v in side:
            values.append(v)
            if n % 2:
                specs.append(VMEM)
            else:
                specs.append(pl.BlockSpec((v.shape[0], tile), lambda i: (0, i)))
    rows = sum(v.shape[0] for v in sides[0])
    return pl.pallas_call(
        partial(grads_kernel, count),
        grid=(inner // tile,),
        in_specs=specs,
        out_specs=pl.BlockSpec((tile, cols), lambda i: (i, 0)),
        out_shape=jax.ShapeDtypeStruct((inner, cols), BF16),
        compiler_params=pltpu.CompilerParams(vmem_limit_bytes=40 << 20),
        cost_estimate=pl.CostEstimate(
            flops=2 * rows * inner * cols,
            bytes_accessed=2 * sum(v.size for v in values) + 2 * inner * cols,
            transcendentals=0,
        ),
    )(*values)


def gelu_pair(preact):
    half = 0.5 + 0.5 * lax.erf(preact * (2.0**-0.5))
    slope = half + preact * jnp.exp(-0.5 * preact * preact) * 0.3989422804014327
    return (preact * half).astype(BF16), slope.astype(BF16)


def body(
    dp,
    seq,
    tokens,
    segment_ids,
    qkv_weight,
    query_bias,
    value_bias,
    out_weight,
    out_bias,
    first_gain,
    first_shift,
    up_weight,
    up_bias,
    down_weight,
    down_bias,
    second_gain,
    second_shift,
    cotangent,
):
    place = Place(dp, seq)
    everyone = dp * seq
    _, count, width = tokens.shape
    hidden_own = up_weight.shape[1] // seq
    heads = HEADS // seq
    head_cols = heads * HEAD_DIM
    shard = qkv_weight.shape[0]
    ff_shard = down_weight.shape[0]
    length = segment_ids.shape[1]
    rows = tokens.reshape(count, width)

    qkv_cols = 3 * head_cols
    smalls = (query_bias, value_bias, out_bias, first_gain, first_shift, down_bias, second_gain, second_shift)
    up_rows = ff_shard // shard
    packed = jnp.concatenate([v.reshape(1, shard) for v in smalls] + [up_bias.reshape(up_rows, shard)])
    vector_count = packed.shape[0]
    qkv_blocks = qkv_weight.reshape(shard, 3, seq, head_cols).transpose(2, 0, 1, 3)
    up_blocks = up_weight.reshape(shard, dp, seq, ff_shard).transpose(2, 0, 1, 3)
    blocks = jnp.concatenate(
        [qkv_blocks.reshape(seq, shard, qkv_cols), up_blocks.reshape(seq, shard, hidden_own)], axis=2
    )
    extra = jnp.pad(packed, ((0, EXTRA - vector_count), (0, blocks.shape[2] - shard)))
    extra = jnp.broadcast_to(extra, (seq, *extra.shape))
    blocks = exchange_seq(place, jnp.concatenate([blocks, extra], axis=1))
    qkv_block = blocks[:, :shard, :qkv_cols].reshape(seq * shard, qkv_cols)
    up_block = blocks[:, :shard, qkv_cols:].reshape(seq * shard, hidden_own)
    packed_seq = blocks[:, shard:, :shard].transpose(1, 0, 2).reshape(EXTRA, seq * shard)
    packed_seq = jnp.pad(packed_seq, ((0, 0), (0, head_cols - seq * shard)))
    out_x = jnp.zeros((place.nx, shard, width), BF16)
    for k in range(place.nx):
        here = out_weight if k == 0 else place.to_x(out_weight, k)
        out_x = put(out_x, here, (place.x - k) % place.nx)
    out_x = out_x.reshape(place.nx * shard, width)

    def columns(a):
        return [a[:, i : i + head_cols] for i in range(0, a.shape[1], head_cols)]

    stack = [(0, b, i * head_cols) for i, b in enumerate(columns(qkv_block))]
    stack += [(1, b, i * head_cols) for i, b in enumerate(columns(out_x))]
    stack += [(2, packed_seq, 0)]
    pieces, at = [], 0
    for i, b, col in stack:
        pieces.append((i, at, b.shape[0], col))
        at += b.shape[0]
    attention = Gather(place, jnp.concatenate([b for _, b, _ in stack], axis=0))
    attention.start()
    for step in range(place.nz - 1):
        attention.settle()
        if step == place.nz - 4:
            early = attention.here
        if step == place.nz - 3:
            middle = attention.here
    up_block, down_block, _ = lax.optimization_barrier((up_block, down_weight, early))
    if hidden_own == width:
        later = lax.all_gather(jnp.concatenate([up_block, down_block], axis=0), "dp", axis=0)
        full_up = later[:, : seq * shard].reshape(width, hidden_own)
        full_down = later[:, seq * shard :].reshape(hidden_own, width)
    else:
        full_up = lax.all_gather(up_block, "dp", axis=0, tiled=True)
        full_down = lax.all_gather(down_block, "dp", axis=0, tiled=True)
    attention.settle()
    full_qkv, packed_all = attention.finish(
        [(i // 2, *rest) for i, *rest in pieces if i != 1], ((seq * shard, qkv_cols), (EXTRA, head_cols))
    )
    (out_half,) = attention.finish(
        [(0, *rest) for i, *rest in pieces if i == 1], ((place.nx * shard, width),)
    )
    out_half = out_half.reshape(dp * place.nx, 1, shard, width)
    full_out = place.pair(out_half, place.core(out_half), 1).reshape(width, width)
    full_qkv = full_qkv.reshape(width, qkv_cols)
    packed_all = packed_all[:, :vector_count, : seq * shard].astype(F32)
    vectors = [packed_all[:, i].reshape(1, width) for i in range(len(smalls))]
    full_query, full_value, bias_out, gain_one, shift_one, bias_down, gain_two, shift_two = vectors
    bias_up = packed_all[:, len(smalls) :].reshape(dp, up_rows, seq, shard)
    bias_up = lax.dynamic_index_in_dim(bias_up, place.s, 2, keepdims=False).reshape(1, hidden_own)

    row_blocks, _ = rows_each(place, rows, lambda k, block: middle)
    all_rows = jnp.zeros((place.nx, CORES * count, width), BF16)
    for k, both in enumerate(row_blocks):
        mine, other = both[:count], both[count:]
        all_rows = put(all_rows, place.pair(mine, other, 0), (place.x + k) % place.nx)
    all_rows = all_rows.reshape(length, width)

    seg_row = segment_ids
    seg_col = segment_ids.reshape(length, 1)
    blocks = length // BLOCK
    ids = segment_ids.reshape(length)
    heads_first = ids[::BLOCK]
    heads_last = ids[BLOCK - 1 :: BLOCK]
    low = jnp.sum(ids[None, :] < heads_first[:, None], axis=1, dtype=jnp.int32)
    high = jnp.sum(ids[None, :] <= heads_last[:, None], axis=1, dtype=jnp.int32)
    bounds = jnp.concatenate([low // BLOCK, (high + BLOCK - 1) // BLOCK])
    own_cols = place.s * head_cols
    query_own = lax.dynamic_slice_in_dim(full_query, own_cols, head_cols, 1)
    value_own = lax.dynamic_slice_in_dim(full_value, own_cols, head_cols, 1)
    qkv_bias = jnp.concatenate([query_own, jnp.zeros_like(query_own), value_own], axis=1)
    qkv = (matmul(all_rows, full_qkv) + qkv_bias).astype(BF16)
    mixed_own, logs = attend(qkv, seg_row, seg_col, bounds, heads)

    mixed = exchange_seq(place, mixed_own.reshape(seq, count, head_cols))
    mixed = mixed.transpose(1, 0, 2).reshape(count, width)
    branch = matmul(mixed, full_out) + bias_out
    first, normed_one, factor_one = norm_forward(rows.astype(F32) + branch, gain_one, shift_one)
    first_low = first.astype(BF16)
    first_all, hidden_slopes = rows_each(
        place, first_low, lambda k, block: gelu_pair(matmul(block, full_up) + bias_up)
    )
    hidden_all = [hidden for hidden, _ in hidden_slopes]
    second = rows_sum(place, hidden_all, lambda hidden: matmul(hidden, full_down)) + bias_down
    result, normed_two, factor_two = norm_forward(first + second, gain_two, shift_two)
    output = result.astype(BF16).reshape(tokens.shape)

    grad_out = cotangent.reshape(count, width).astype(F32)
    second_grad, gain_two_grad, shift_two_grad = norm_backward(
        grad_out, normed_two, factor_two, gain_two
    )
    second_low = second_grad.astype(BF16)
    down_bias_grad = jnp.sum(second_low, axis=0, dtype=F32)
    second_all, preact_all = rows_each(
        place,
        second_low,
        lambda k, block: (
            right_product(block, full_down) * hidden_slopes[k][1].astype(F32)
        ).astype(BF16),
    )
    if hidden_own == width:
        beside = weight_grads(hidden_all, second_all, first_all, preact_all)
        both_owned = lax.psum_scatter(beside, "dp", scatter_dimension=0, tiled=True)
        down_owned, up_owned = both_owned[:, :width].astype(F32), both_owned[:, width:]
    else:
        down_grad = weight_grads(hidden_all, second_all)
        down_owned = lax.psum_scatter(down_grad, "dp", scatter_dimension=0, tiled=True).astype(F32)
        beside = weight_grads(first_all, preact_all)
        up_owned = lax.psum_scatter(beside, "dp", scatter_dimension=0, tiled=True)
    first_grad = second_grad + rows_sum(
        place, preact_all, lambda p: right_product(p, full_up), beside
    )
    up_bias_grad = sum(jnp.sum(p, axis=0, dtype=F32) for p in preact_all)

    residual_grad, gain_one_grad, shift_one_grad = norm_backward(
        first_grad, normed_one, factor_one, gain_one
    )
    branch_low = residual_grad.astype(BF16)
    out_bias_grad = jnp.sum(branch_low, axis=0, dtype=F32)
    mixed_grad = right_product(branch_low, full_out).astype(BF16)
    grad_blocks = mixed_grad.reshape(count, seq, head_cols).transpose(1, 0, 2)
    grad_own = exchange_seq(place, grad_blocks).reshape(length, head_cols)

    up_bias_wide = lax.dynamic_update_index_in_dim(
        jnp.zeros((dp, seq, ff_shard), F32), up_bias_grad.reshape(dp, ff_shard), place.s, 1
    ).reshape(everyone, ff_shard)
    vector_sums = (
        out_bias_grad,
        gain_one_grad,
        shift_one_grad,
        down_bias_grad,
        gain_two_grad,
        shift_two_grad,
    )
    extra = jnp.concatenate([v.reshape(everyone, shard) for v in vector_sums] + [up_bias_wide], axis=1)
    wide_count = extra.shape[1]
    extra = jnp.pad(extra.astype(BF16)[:, None], ((0, 0), (0, EXTRA - 1), (0, width - wide_count)))
    branch_late, _ = lax.optimization_barrier((branch_low, mixed_grad))
    out_grad = weight_grads([mixed], [branch_late]).reshape(everyone, shard, width)
    view = jnp.concatenate([out_grad, extra], axis=1)
    view = view.reshape(dp * place.nx, CORES, shard + EXTRA, width)
    mine = lax.dynamic_index_in_dim(view, place.c, 1, keepdims=False)
    other = lax.dynamic_index_in_dim(view, 1 - place.c, 1, keepdims=False)
    view = (mine.astype(F32) + place.core(other).astype(F32)).astype(BF16)
    view = view.reshape(dp, place.nx, shard + EXTRA, width)
    summed = lax.dynamic_index_in_dim(view, place.x, 1, keepdims=False).astype(F32)
    for k in range(1, place.nx):
        sent = lax.dynamic_index_in_dim(view, (place.x + k) % place.nx, 1, keepdims=False)
        summed = summed + place.to_x(sent, k).astype(F32)
    qkv_grad = attend_back(qkv, mixed_own, grad_own, logs, seg_row, seg_col, bounds, heads)
    qkv_grad, summed = lax.optimization_barrier((qkv_grad, summed))
    token_parts = right_product(qkv_grad, full_qkv).astype(BF16)
    token_parts = token_parts.reshape(place.nx, CORES, count, width)
    ordered = []
    for k in range(place.nx):
        both = take(token_parts, (place.x + k) % place.nx)
        ordered.append(
            jnp.concatenate([take(both, place.c), take(both, 1 - place.c)], axis=0)
        )
    token_sum = rows_sum(place, ordered, lambda v: v)
    joint_grad = weight_grads([all_rows], [qkv_grad])

    joint_grad = joint_grad.reshape(dp, seq * shard, qkv_cols)
    sums = jnp.sum(qkv_grad, axis=0, dtype=F32).reshape(3, head_cols)
    ends = jnp.stack([sums[0], sums[2]])
    ends = lax.dynamic_update_slice_in_dim(jnp.zeros((2, width), F32), ends, own_cols, 1)
    ends = ends.reshape(2, dp, seq * shard).transpose(1, 0, 2).reshape(dp, 1, 2 * seq * shard)
    ends = jnp.pad(ends.astype(BF16), ((0, 0), (0, EXTRA - 1), (0, head_cols - 2 * seq * shard)))
    views = [(joint_grad, i * head_cols, head_cols) for i in range(3)]
    views += [(ends, 0, head_cols)]
    views += [(summed.astype(BF16), i, head_cols) for i in range(0, width, head_cols)]
    owned = scatter_dp(place, views, token_sum)
    per = seq * shard
    joint = jnp.concatenate([owned[i * per : (i + 1) * per] for i in range(3)], axis=1).astype(BF16)
    ends = owned[3 * per]
    owned = owned[3 * per + EXTRA :].reshape(-1, shard + EXTRA, head_cols)
    out_owned = owned[:, :shard].transpose(1, 0, 2).reshape(shard, width)
    wide = owned[:, shard].reshape(width)
    out_bias_owned, gain_one_owned, shift_one_owned, down_bias_owned, gain_two_owned, shift_two_owned = [
        wide[i * shard : (i + 1) * shard] for i in range(len(vector_sums))
    ]
    up_bias_owned = wide[len(vector_sums) * shard : wide_count]
    ends = ends[: 2 * per].astype(BF16).reshape(2, seq, shard).transpose(1, 0, 2)
    ends = jnp.pad(
        ends.reshape(seq, 1, 2 * shard), ((0, 0), (0, EXTRA - 1), (0, qkv_cols - 2 * shard))
    )
    joint = jnp.concatenate([joint.reshape(seq, shard, qkv_cols), ends], axis=1)
    joint = exchange_seq(place, joint)
    up_owned, joint = lax.optimization_barrier((up_owned, joint))
    up_owned = up_owned.reshape(seq, shard, hidden_own)
    up_owned = exchange_seq(place, up_owned).reshape(seq, shard, dp, ff_shard)
    up_owned = up_owned.transpose(1, 2, 0, 3).reshape(up_weight.shape).astype(F32)
    joint_owned = joint[:, :shard].reshape(seq, shard, 3, head_cols).transpose(1, 2, 0, 3)
    joint_owned = joint_owned.reshape(qkv_weight.shape).astype(F32)
    ends = jnp.sum(joint[:, shard, : 2 * shard].astype(F32), axis=0).reshape(2, shard)

    tokens_grad = (residual_grad + token_sum).astype(BF16).reshape(tokens.shape)
    return (
        output,
        tokens_grad,
        joint_owned,
        ends[0],
        ends[1],
        out_owned,
        out_bias_owned,
        gain_one_owned,
        shift_one_owned,
        up_owned,
        up_bias_owned,
        down_owned,
        down_bias_owned,
        gain_two_owned,
        shift_two_owned,
    )


def solution(mesh):
    rows = P("dp", "seq", None)
    matrix = P(("dp", "seq"), None)
    vector = P(("dp", "seq"))
    params = (
        matrix,
        vector,
        vector,
        matrix,
        vector,
        vector,
        vector,
        matrix,
        vector,
        matrix,
        vector,
        vector,
        vector,
    )
    return jax.shard_map(
        partial(body, mesh.shape["dp"], mesh.shape["seq"]),
        mesh=mesh,
        in_specs=(rows, P("dp", None), *params, rows),
        out_specs=(rows, rows, *params),
        check_vma=False,
    )
```
